32 devices in a mesh: groups: 1, chain: 4 (over y, x), tm: 8 (over z, core).
Axes of the slice: x: 2, y: 2, z: 4, core: 2. Of those that a mesh axis runs over, the one named last changes fastest.
Arguments:
- traces: bfloat16 [4, 2048, 1024], P(('groups', 'chain'), 'tm'), may hold values from -100 to 100
- lengths: int32 [4], P('groups'), may hold values from 1024 to 1793, as said below
Outputs:
- omega: float32 [1024, 1024], P(('groups', 'chain', 'tm'))
The draws below stay inside these ranges and needn't reach their ends.
Inputs may be any that keep to these rules, and one draw needn't show every extreme that they name: `lengths`: every chain has between half of the window and 1793 valid draws; some chain has exactly each of the two ends.
All inputs are finite; a program needn't handle non-finite values.
Results may differ from the reference program's by a relative error of at most 0.0003.
Values may be sent and summed in bfloat16 or wider, within the bound.
A program may use at most 64 MiB of HBM per device.

```python
import math
import jax
import jax.numpy as jnp
from jax import lax

P_SIZE = 1024
LAG = 256
CHAINS = 4
TIME = 2048


def draw_traces(key, part):
    key_scale = jax.random.fold_in(key, 11)
    key_noise = jax.random.fold_in(key, 12)
    key_level = jax.random.fold_in(key, 13)
    key_sign = jax.random.fold_in(key, 14)
    spread = jnp.exp(jax.random.uniform(key_scale, (P_SIZE,), jnp.float32, 0.0, math.log(10.0)))
    noise = jnp.clip(jax.random.normal(key_noise, (CHAINS, TIME, P_SIZE), jnp.float32), -6.0, 6.0)
    level = jax.random.uniform(key_level, (CHAINS, 1, P_SIZE), jnp.float32, 1.0, 3.0)
    sign = jnp.where(jax.random.uniform(key_sign, (CHAINS, 1, P_SIZE), jnp.float32) < 0.5, -1.0, 1.0)
    ramp = 0.5 + jnp.arange(TIME).astype(jnp.float32) / TIME
    values = level * sign * ramp[None, :, None] + spread[None, None, :] * noise
    return values.astype(jnp.bfloat16)


def draw_lengths(key, part):
    key_body = jax.random.fold_in(key, 21)
    key_first = jax.random.fold_in(key, 22)
    key_second = jax.random.fold_in(key, 23)
    values = jax.random.randint(key_body, (CHAINS,), TIME // 2, TIME - LAG + 2, jnp.int32)
    first = jax.random.randint(key_first, (), 0, CHAINS, jnp.int32)
    offset = jax.random.randint(key_second, (), 1, CHAINS, jnp.int32)
    second = (first + offset) % CHAINS
    index = jnp.arange(CHAINS, dtype=jnp.int32)
    values = jnp.where(index == first, TIME - LAG + 1, values)
    values = jnp.where(index == second, TIME // 2, values)
    return values.astype(jnp.int32)


def setup_inputs(seed: int = 0, part: int = 0) -> dict:
    seeds = jax.random.split(jax.random.key(seed), 3)
    part_splits = jax.random.split(jax.random.fold_in(seeds[2], part), 3)
    traces = draw_traces(jax.random.fold_in(jax.random.fold_in(seeds[2], part), 71), part)
    lengths = draw_lengths(jax.random.fold_in(jax.random.fold_in(seeds[2], part), 71), part)
    return {"traces": traces, "lengths": lengths}


def window_sums(current, previous):
    chains, steps, width = current.shape
    count = steps // LAG
    blocks = current.reshape(chains, count, LAG, width)
    earlier = jnp.concatenate([previous[:, None], blocks[:, :-1]], axis=1)
    index = jnp.arange(LAG)
    lower = (index[None, :] <= index[:, None]).astype(jnp.float32)
    upper = (index[None, :] > index[:, None]).astype(jnp.float32)
    result = jnp.einsum("ij,cbjp->cbip", lower, blocks, precision=lax.Precision.HIGHEST)
    result = result + jnp.einsum("ij,cbjp->cbip", upper, earlier, precision=lax.Precision.HIGHEST)
    return result.reshape(chains, steps, width)


def reference(traces, lengths):
    def one_chain(total, item):
        trace, length = item
        valid = (jnp.arange(TIME) < length).astype(jnp.float32)[:, None]
        data = trace.astype(jnp.float32) * valid
        mean = jnp.sum(data, axis=0) / length.astype(jnp.float32)
        centered = (data - mean[None, :]) * valid
        filtered = window_sums(centered[None], jnp.zeros((1, LAG, P_SIZE), jnp.float32))[0]
        product = jnp.einsum("tk,tp->kp", filtered, filtered, precision=lax.Precision.HIGHEST)
        return total + product, None

    start = jnp.zeros((P_SIZE, P_SIZE), jnp.float32)
    total, _ = lax.scan(one_chain, start, (traces, lengths))
    scale = 1.0 / (LAG * jnp.sum(lengths).astype(jnp.float32))
    return total * scale
```

```python
import functools

import jax
import jax.numpy as jnp
from jax import lax
from jax.experimental import pallas as pl
from jax.experimental.pallas import tpu as pltpu
from jax.sharding import PartitionSpec as P

LAG = 256
MESH = pl.DeviceIdType.MESH


def shifted(block, axis, distance):
    devices = range(lax.axis_size(axis))
    route = [(i - distance, i) for i in devices if i - distance in devices]
    return lax.ppermute(block, axis, route)


def window_sums(current, previous):
    chains, steps, width = current.shape
    count = steps // LAG
    blocks = current.reshape(chains, count, LAG, width)
    earlier = jnp.concatenate([previous[:, None], blocks[:, :-1]], axis=1)
    index = jnp.arange(LAG)
    lower = index[None, :] <= index[:, None]
    upper = index[None, :] > index[:, None]
    lower_mat = lower.astype(jnp.float32)
    upper_mat = upper.astype(jnp.float32)
    result = jnp.einsum("ij,cbjp->cbip", lower_mat, blocks, precision=lax.Precision.HIGHEST)
    result = result + jnp.einsum(
        "ij,cbjp->cbip", upper_mat, earlier, precision=lax.Precision.HIGHEST
    )
    return result.reshape(chains, steps, width)


def gram_rows(filtered):
    chains, steps, width = filtered.shape
    flat = filtered.reshape(chains * steps, width)
    return jnp.einsum("tk,tp->kp", flat, flat, precision=lax.Precision.HIGHEST)


def on_device(traces, lengths):
    chains, steps, width = traces.shape
    own_len = lax.dynamic_slice_in_dim(lengths, lax.axis_index("chain") * chains, chains)
    first_time = lax.axis_index("tm") * steps
    times = first_time + jnp.arange(steps, dtype=jnp.int32)
    valid = (times[None, :] < own_len[:, None]).astype(jnp.float32)
    back_times = times - steps
    back_valid = ((back_times[None, :] >= 0) & (back_times[None, :] < own_len[:, None])).astype(
        jnp.float32
    )
    behind = shifted(traces, "tm", 1)
    data = traces.astype(jnp.float32) * valid[..., None]
    earlier = behind.astype(jnp.float32) * back_valid[..., None]
    totals = lax.psum(jnp.sum(data, axis=1), "tm")
    mean = totals / own_len.astype(jnp.float32)[:, None]
    scale = 1.0 / (LAG * jnp.sum(lengths).astype(jnp.float32))
    centered = window_sums(
        (data - mean[:, None, :]) * valid[..., None],
        (earlier - mean[:, None, :]) * back_valid[..., None],
    )
    return lax.psum_scatter(
        scale * gram_rows(centered), ("chain", "tm"), scatter_dimension=0, tiled=True
    )


def dot(a, b):
    return jnp.dot(a, b, preferred_element_type=jnp.float32)


NQ = 4
TOP = 32767.0


def kernel(
    len_hbm, x_hbm, o_ref, len_ref, data, ext, hi_e, lo_e, hi_et, lo_et, sums, hi, lo, hi_t, lo_t, keep, code1, scale1, got1,
    gots1, code2, scale2, got2, gots2, plane, code3, scale3, got3, gots3, in_sem, s_sum, r_sum, s_x, r_x,
    s_halo, r_halo, s_fwd, r_fwd, s1, r1, s1s,
    r1s, s2, r2, s2s, r2s, s3, r3, s3s, r3s,
):
    steps, width = x_hbm.shape
    pad = steps // 2
    half = width // 2
    cols = half // NQ
    rows = width // 4
    orows = rows // 8
    c = lax.axis_index("chain")
    k = lax.axis_index("tm")
    z = k // 2
    j = k % 2

    def copy(src, dst, send, recv, **where):
        return pltpu.make_async_remote_copy(
            src_ref=src, dst_ref=dst, send_sem=send, recv_sem=recv, device_id=where,
            device_id_type=MESH,
        )

    def start(copies):
        for cp in copies:
            cp.start()

    def arrive(copies):
        for cp in copies:
            cp.wait_recv()

    own = pl.ds(pl.multiple_of(pad + steps * j, pad), steps)
    len_in = pltpu.make_async_copy(len_hbm, len_ref, in_sem.at[0])
    x_in = pltpu.make_async_copy(x_hbm, data.at[own, :], in_sem.at[1])
    len_in.start()
    x_in.start()
    barrier = pltpu.get_barrier_semaphore()
    for r in range(1, 8):
        pl.semaphore_signal(barrier, inc=1, device_id={"tm": k ^ r}, device_id_type=MESH)
    for r in (1, 2):
        pl.semaphore_signal(barrier, inc=1, device_id={"chain": c ^ r}, device_id_type=MESH)

    len_in.wait()
    length = len_ref[c]
    total_len = len_ref[0]
    for i in range(1, len_ref.shape[0]):
        total_len = total_len + len_ref[i]
    scale = 1.0 / (LAG * jnp.full((1, 1), total_len, jnp.int32).astype(jnp.float32))

    time = k * steps + lax.broadcasted_iota(jnp.int32, (steps, 1), 0)
    valid = (time < length).astype(jnp.float32)
    x_in.wait()
    sums[0] = jnp.sum(data[own, :].astype(jnp.float32) * valid, axis=0, keepdims=True)

    @pl.when(z == 0)
    def _():
        data[0:pad, :] = jnp.zeros((pad, width), data.dtype)

    @pl.when(z == 3)
    def _():
        data[5 * pad : 6 * pad, :] = jnp.zeros((pad, width), data.dtype)

    pl.semaphore_wait(barrier, 9)

    sum_copies = [
        copy(sums.at[0], sums.at[r], s_sum.at[r], r_sum.at[r], tm=k ^ r) for r in range(1, 8)
    ]
    for cp in sum_copies:
        cp.start()
    def halo(way, h):
        near = 2 * jnp.minimum(z + 1, 3) if way == 0 else 2 * jnp.maximum(z - 1, 0)
        take = 4 * pad if way == 0 else pad
        put = 0 if way == 0 else 5 * pad
        at = pl.ds(half * h, half)
        return copy(
            data.at[pl.ds(take, pad), at], data.at[pl.ds(put, pad), at], s_halo.at[h],
            r_halo.at[way], tm=near + h,
        )

    ups = [halo(0, h) for h in range(2)]
    downs = [halo(1, h) for h in range(2)]

    @pl.when((j == 1) & (z < 3))
    def _():
        start(ups)

    @pl.when((j == 0) & (z > 0))
    def _():
        start(downs)

    x_copy = copy(data.at[own, :], data.at[own, :], s_x, r_x, tm=k ^ 1)
    x_copy.start()

    mine = pl.ds(pl.multiple_of(half * j, half), half)
    forwards, landed = [], []
    for way, put in ((0, 0), (1, 5 * pad)):
        block = data.at[pl.ds(put, pad), mine]
        forwards.append(copy(block, block, s_fwd.at[way], r_fwd.at[way], tm=k ^ 1))
        landed.append(copy(block, block, s_halo.at[0], r_halo.at[way], tm=k ^ 1))

    @pl.when(z > 0)
    def _():
        landed[0].wait_recv()
        forwards[0].start()

    @pl.when(z < 3)
    def _():
        landed[1].wait_recv()
        forwards[1].start()

    i_idx = lax.broadcasted_iota(jnp.int32, (steps, 2 * steps), 0)
    r_idx = lax.broadcasted_iota(jnp.int32, (steps, 2 * steps), 1)
    for cp in sum_copies:
        cp.wait_recv()
    total = sums[0]
    for r in range(1, 8):
        total = total + sums[r]
    mean = total / jnp.full((1, 1), length, jnp.int32).astype(jnp.float32)

    def windows(b):
        first = 2 * steps * z + pad + steps * b
        when = first - steps + r_idx
        keep = (r_idx > i_idx) & (r_idx <= i_idx + LAG) & (when >= 0) & (when < length)
        band = keep.astype(jnp.float32).astype(jnp.bfloat16)
        t = first + lax.broadcasted_iota(jnp.int32, (steps, 1), 0)
        count = jnp.maximum(
            jnp.minimum(t + 1, length) - jnp.maximum(t - (LAG - 1), 0), 0
        ).astype(jnp.float32)
        out = slice(steps * b, steps * (b + 1))
        for n in range(width // 256):
            at = slice(256 * n, 256 * (n + 1))
            w = dot(band, data[steps * b : steps * (b + 2), at]) - count * mean[:, at]
            h = w.astype(jnp.bfloat16)
            e = (w - h.astype(jnp.float32)).astype(jnp.bfloat16)
            hi[out, at] = h
            lo[out, at] = e
            hi_t[at, out] = h.T
            lo_t[at, out] = e.T

    x_copy.wait_recv()

    @pl.when(z == 0)
    def _():
        row = lax.broadcasted_iota(jnp.int32, (pad, pad), 0)
        col = lax.broadcasted_iota(jnp.int32, (pad, pad), 1)
        band = ((col <= row) & (col < length)).astype(jnp.float32).astype(jnp.bfloat16)
        t = lax.broadcasted_iota(jnp.int32, (pad, 1), 0)
        count = jnp.minimum(t + 1, length).astype(jnp.float32)
        for n in range(width // 256):
            at = slice(256 * n, 256 * (n + 1))
            w = dot(band, data[pad : 2 * pad, at]) - count * mean[:, at]
            h = w.astype(jnp.bfloat16)
            e = (w - h.astype(jnp.float32)).astype(jnp.bfloat16)
            hi_e[:, at] = h
            lo_e[:, at] = e
            hi_et[at, :] = h.T
            lo_et[at, :] = e.T
        for p in range(NQ // 2):
            at = pl.ds(pl.multiple_of(half * j + 2 * cols * p, 2 * cols), 2 * cols)
            for r in range(4):
                left = pl.ds(pl.multiple_of(rows * (c ^ r), rows), rows)
                ext[p, r] = (
                    dot(hi_et[left, :], lo_e[:, at])
                    + dot(lo_et[left, :], hi_e[:, at])
                    + dot(hi_et[left, :], hi_e[:, at])
                )

    @pl.when(z != 0)
    def _():
        ext[...] = jnp.zeros_like(ext)

    @pl.when(z > 0)
    def _():
        forwards[0].wait_recv()

    windows(0)

    @pl.when(z < 3)
    def _():
        forwards[1].wait_recv()

    windows(1)

    def send(codes, scales, to_codes, to_scales, sems, at, **where):
        (sc, rc), (ss, rs) = sems
        return [
            copy(codes, to_codes, sc.at[at], rc.at[at], **where),
            copy(scales, to_scales, ss.at[at], rs.at[at], **where),
        ]

    def pack(values, codes, scales, at, flat=False):
        for g in range(8):
            v = values(g)
            top = jnp.maximum(jnp.max(jnp.abs(v), axis=0, keepdims=True), 1e-33)
            place = (g,) if flat else (g // 2, slice(g % 2, g % 2 + 1))
            scales[(*at, *place)] = top * (1.0 / TOP)
            code = jnp.round(v * (TOP / top)).astype(jnp.int32).astype(jnp.int16)
            codes[(*at, slice(32 * g, 32 * g + 32))] = code

    def unpack(codes, scales, at, g):
        code = codes[(*at, slice(32 * g, 32 * g + 32))].astype(jnp.int32).astype(jnp.float32)
        return code * scales[(*at, g // 2, slice(g % 2, g % 2 + 1))]

    first_hop, second_hop, z_hops = [], [], []

    def goal(i):
        return k ^ i

    for q in range(NQ):
        m1 = 1 + q % 2
        m2 = 3 - m1
        first_hop.append([
            send(
                code1.at[q, i], scale1.at[q, i], got1.at[q, i], gots1.at[q, i],
                ((s1, r1), (s1s, r1s)), (q, i), chain=c ^ m1,
            )
            for i in range(2)
        ])
        second_hop.append(
            send(
                code2.at[q], scale2.at[q], got2.at[q], gots2.at[q], ((s2, r2), (s2s, r2s)), q,
                chain=c ^ m2,
            )
        )
        z_hops.append([
            send(
                code3.at[q, pl.ds(pl.multiple_of(goal(i) * orows, orows), orows), :],
                scale3.at[q, goal(i)], got3.at[q, i - 1], gots3.at[q, i - 1],
                ((s3, r3), (s3s, r3s)), (q, i - 1), tm=k ^ i,
            )
            for i in range(1, 8)
        ])

    def hop2(q):
        arrive(first_hop[q][1])
        pack(
            lambda g: keep[q, 1, 32 * g : 32 * g + 32] + unpack(got1, gots1, (q, 1), g),
            code2, scale2, (q,),
        )
        start(second_hop[q])

    def hop3(q):
        arrive(first_hop[q][0])
        arrive(second_hop[q])

        def value(g):
            v = (
                keep[q, 0, 32 * g : 32 * g + 32]
                + unpack(got1, gots1, (q, 0), g)
                + unpack(got2, gots2, (q,), g)
            )
            plane[q, 32 * g : 32 * g + 32] = v
            return v

        pack(value, code3, scale3, (q,), True)
        for copies in z_hops[q]:
            start(copies)

    def hop4(q):
        here = plane[q, pl.ds(pl.multiple_of(orows * k, orows), orows), :]
        there = None
        for i in (2, 4, 6, 1, 3, 5, 7):
            arrive(z_hops[q][i - 1])
            v = got3[q, i - 1].astype(jnp.int32).astype(jnp.float32) * gots3[q, i - 1]
            if i % 2 == 0:
                here = here + v
            else:
                there = v if there is None else there + v
        o_ref[:, pl.ds(pl.multiple_of(half * j + cols * q, cols), cols)] = here * scale
        o_ref[:, pl.ds(pl.multiple_of(half * (1 - j) + cols * q, cols), cols)] = there * scale

    def products(p, go):
        at = pl.ds(pl.multiple_of(half * j + 2 * cols * p, 2 * cols), 2 * cols)
        right_hi = hi[:, at]
        right_lo = lo[:, at]
        for r in (3, 1, 2, 0):
            left = pl.ds(pl.multiple_of(rows * (c ^ r), rows), rows)
            w = (
                dot(hi_t[left, :], right_lo)
                + dot(lo_t[left, :], right_hi)
                + dot(hi_t[left, :], right_hi)
                + ext[p, r]
            )
            for b in range(2):
                q = 2 * p + b
                part = w[:, cols * b : cols * (b + 1)]
                if r == 3 or r == 1 + b:
                    slot = int(r == 3)
                    pack(lambda g: part[32 * g : 32 * g + 32], code1, scale1, (q, slot))
                    if go:
                        start(first_hop[q][slot])
                else:
                    keep[q, int(r != 0)] = part

    products(0, True)
    products(1, False)
    hop2(0)
    hop2(1)
    for i in (1, 0):
        start(first_hop[2][i])
        start(first_hop[3][i])
    hop3(0)
    hop3(1)
    hop2(2)
    hop2(3)
    hop3(2)
    hop3(3)
    for q in range(NQ):
        hop4(q)
    for cp in sum_copies:
        cp.wait_send()
    x_copy.wait_send()

    @pl.when((j == 1) & (z < 3))
    def _():
        for cp in ups:
            cp.wait_send()

    @pl.when((j == 0) & (z > 0))
    def _():
        for cp in downs:
            cp.wait_send()

    @pl.when(z > 0)
    def _():
        forwards[0].wait_send()

    @pl.when(z < 3)
    def _():
        forwards[1].wait_send()

    for q in range(NQ):
        for copies in (*first_hop[q], second_hop[q], *z_hops[q]):
            for cp in copies:
                cp.wait_send()


def hbm(x):
    return pltpu.with_memory_space_constraint(x, pltpu.HBM)


def fused(traces, lengths):
    _, steps, width = traces.shape
    f32, bf16, i16 = jnp.float32, jnp.bfloat16, jnp.int16
    rows, cols = width // 4, width // 2 // NQ
    dma = pltpu.SemaphoreType.DMA
    return pl.pallas_call(
        kernel,
        out_shape=jax.ShapeDtypeStruct((width // 32, width), f32),
        in_specs=[
            pl.BlockSpec(memory_space=pltpu.HBM),
            pl.BlockSpec(memory_space=pltpu.HBM),
        ],
        out_specs=pl.BlockSpec(memory_space=pltpu.VMEM),
        scratch_shapes=[
            pltpu.SMEM(lengths.shape, jnp.int32),
            pltpu.VMEM((3 * steps, width), bf16),
            pltpu.VMEM((NQ // 2, 4, rows, 2 * cols), f32),
            pltpu.VMEM((steps // 2, width), bf16),
            pltpu.VMEM((steps // 2, width), bf16),
            pltpu.VMEM((width, steps // 2), bf16),
            pltpu.VMEM((width, steps // 2), bf16),
            pltpu.VMEM((8, 1, width), f32),
            pltpu.VMEM((2 * steps, width), bf16),
            pltpu.VMEM((2 * steps, width), bf16),
            pltpu.VMEM((width, 2 * steps), bf16),
            pltpu.VMEM((width, 2 * steps), bf16),
            pltpu.VMEM((NQ, 2, rows, cols), f32),
            pltpu.VMEM((NQ, 2, rows, cols), i16),
            pltpu.VMEM((NQ, 2, 4, 2, cols), f32),
            pltpu.VMEM((NQ, 2, rows, cols), i16),
            pltpu.VMEM((NQ, 2, 4, 2, cols), f32),
            pltpu.VMEM((NQ, rows, cols), i16),
            pltpu.VMEM((NQ, 4, 2, cols), f32),
            pltpu.VMEM((NQ, rows, cols), i16),
            pltpu.VMEM((NQ, 4, 2, cols), f32),
            pltpu.VMEM((NQ, rows, cols), f32),
            pltpu.VMEM((NQ, rows, cols), i16),
            pltpu.VMEM((NQ, 8, 1, cols), f32),
            pltpu.VMEM((NQ, 7, rows // 8, cols), i16),
            pltpu.VMEM((NQ, 7, 1, cols), f32),
            dma((2,)),
            dma((8,)), dma((8,)),
            dma, dma,
            dma((2,)), dma((2,)),
            dma((2,)), dma((2,)),
            dma((NQ, 2)), dma((NQ, 2)), dma((NQ, 2)), dma((NQ, 2)),
            dma((NQ,)), dma((NQ,)), dma((NQ,)), dma((NQ,)),
            dma((NQ, 7)), dma((NQ, 7)), dma((NQ, 7)), dma((NQ, 7)),
        ],
        compiler_params=pltpu.CompilerParams(
            collective_id=0, has_side_effects=True, vmem_limit_bytes=24 * 2**20
        ),
    )(hbm(lengths), hbm(traces.reshape(steps, width)))


def body(mesh, traces, lengths):
    chains, steps, width = traces.shape
    laid_out = (
        mesh.shape["groups"] == 1 and mesh.shape["chain"] == 4 and mesh.shape["tm"] == 8
    )
    if laid_out and chains == 1 and steps == LAG and width == 1024:
        return fused(traces, lengths)
    return on_device(traces, lengths)


def solution(mesh):
    in_specs = (P(("groups", "chain"), "tm", None), P("groups"))
    out_specs = P(("groups", "chain", "tm"), None)
    return jax.shard_map(
        functools.partial(body, mesh), mesh=mesh, in_specs=in_specs, out_specs=out_specs,
        check_vma=False,
    )
```

```python
import functools

import jax
import jax.numpy as jnp
from jax import lax
from jax.experimental import pallas as pl
from jax.experimental.pallas import tpu as pltpu
from jax.sharding import PartitionSpec as P

LAG = 256
MESH = pl.DeviceIdType.MESH


def shifted(block, axis, distance):
    devices = range(lax.axis_size(axis))
    route = [(i - distance, i) for i in devices if i - distance in devices]
    return lax.ppermute(block, axis, route)


def window_sums(current, previous):
    chains, steps, width = current.shape
    count = steps // LAG
    blocks = current.reshape(chains, count, LAG, width)
    earlier = jnp.concatenate([previous[:, None], blocks[:, :-1]], axis=1)
    index = jnp.arange(LAG)
    lower = index[None, :] <= index[:, None]
    upper = index[None, :] > index[:, None]
    lower_mat = lower.astype(jnp.float32)
    upper_mat = upper.astype(jnp.float32)
    result = jnp.einsum("ij,cbjp->cbip", lower_mat, blocks, precision=lax.Precision.HIGHEST)
    result = result + jnp.einsum(
        "ij,cbjp->cbip", upper_mat, earlier, precision=lax.Precision.HIGHEST
    )
    return result.reshape(chains, steps, width)


def gram_rows(filtered):
    chains, steps, width = filtered.shape
    flat = filtered.reshape(chains * steps, width)
    return jnp.einsum("tk,tp->kp", flat, flat, precision=lax.Precision.HIGHEST)


def on_device(traces, lengths):
    chains, steps, width = traces.shape
    own_len = lax.dynamic_slice_in_dim(lengths, lax.axis_index("chain") * chains, chains)
    first_time = lax.axis_index("tm") * steps
    times = first_time + jnp.arange(steps, dtype=jnp.int32)
    valid = (times[None, :] < own_len[:, None]).astype(jnp.float32)
    back_times = times - steps
    back_valid = ((back_times[None, :] >= 0) & (back_times[None, :] < own_len[:, None])).astype(
        jnp.float32
    )
    behind = shifted(traces, "tm", 1)
    data = traces.astype(jnp.float32) * valid[..., None]
    earlier = behind.astype(jnp.float32) * back_valid[..., None]
    totals = lax.psum(jnp.sum(data, axis=1), "tm")
    mean = totals / own_len.astype(jnp.float32)[:, None]
    scale = 1.0 / (LAG * jnp.sum(lengths).astype(jnp.float32))
    centered = window_sums(
        (data - mean[:, None, :]) * valid[..., None],
        (earlier - mean[:, None, :]) * back_valid[..., None],
    )
    return lax.psum_scatter(
        scale * gram_rows(centered), ("chain", "tm"), scatter_dimension=0, tiled=True
    )


def dot(a, b):
    return jnp.dot(a, b, preferred_element_type=jnp.float32)


NQ = 4
TOP = 32767.0


def kernel(
    len_hbm, x_hbm, o_ref, len_ref, data, ext, hi_e, lo_e, hi_et, lo_et, sums, hi, lo, hi_t, lo_t, keep, code1, scale1, got1,
    gots1, code2, scale2, got2, gots2, plane, code3, scale3, got3, gots3, mean_ref, in_sem, s_sum, r_sum, s_x, r_x,
    s_halo, r_halo, s_fwd, r_fwd, s1, r1, s1s,
    r1s, s2, r2, s2s, r2s, s3, r3, s3s, r3s,
):
    steps, width = x_hbm.shape
    pad = steps // 2
    half = width // 2
    cols = half // NQ
    rows = width // 4
    part = rows // 2
    orows = rows // 8
    c = lax.axis_index("chain")
    k = lax.axis_index("tm")
    z = k // 2
    j = k % 2

    def copy(src, dst, send, recv, **where):
        return pltpu.make_async_remote_copy(
            src_ref=src, dst_ref=dst, send_sem=send, recv_sem=recv, device_id=where,
            device_id_type=MESH,
        )

    def start(copies):
        for cp in copies:
            cp.start()

    def arrive(copies):
        for cp in copies:
            cp.wait_recv()

    own = pl.ds(pl.multiple_of(pad + steps * j, pad), steps)
    len_in = pltpu.make_async_copy(len_hbm, len_ref, in_sem.at[0])
    x_in = pltpu.make_async_copy(x_hbm, data.at[own, :], in_sem.at[1])
    len_in.start()
    x_in.start()
    barrier = pltpu.get_barrier_semaphore()
    for r in range(1, 8):
        pl.semaphore_signal(barrier, inc=1, device_id={"tm": k ^ r}, device_id_type=MESH)
    for r in (1, 2):
        pl.semaphore_signal(barrier, inc=1, device_id={"chain": c ^ r}, device_id_type=MESH)

    len_in.wait()
    length = len_ref[c]
    total_len = len_ref[0]
    for i in range(1, len_ref.shape[0]):
        total_len = total_len + len_ref[i]
    scale = 1.0 / (LAG * jnp.full((1, 1), total_len, jnp.int32).astype(jnp.float32))

    time = k * steps + lax.broadcasted_iota(jnp.int32, (steps, 1), 0)
    valid = (time < length).astype(jnp.float32)
    x_in.wait()
    sums[0] = jnp.sum(data[own, :].astype(jnp.float32) * valid, axis=0, keepdims=True)

    @pl.when(z == 0)
    def _():
        data[0:pad, :] = jnp.zeros((pad, width), data.dtype)

    @pl.when(z == 3)
    def _():
        data[5 * pad : 6 * pad, :] = jnp.zeros((pad, width), data.dtype)

    pl.semaphore_wait(barrier, 9)

    sum_copies = [
        copy(sums.at[0], sums.at[r], s_sum.at[r], r_sum.at[r], tm=k ^ r) for r in range(1, 8)
    ]
    for cp in sum_copies:
        cp.start()
    def halo(way, h):
        near = 2 * jnp.minimum(z + 1, 3) if way == 0 else 2 * jnp.maximum(z - 1, 0)
        take = 4 * pad if way == 0 else pad
        put = 0 if way == 0 else 5 * pad
        at = pl.ds(half * h, half)
        return copy(
            data.at[pl.ds(take, pad), at], data.at[pl.ds(put, pad), at], s_halo.at[h],
            r_halo.at[way], tm=near + h,
        )

    ups = [halo(0, h) for h in range(2)]
    downs = [halo(1, h) for h in range(2)]

    @pl.when((j == 1) & (z < 3))
    def _():
        start(ups)

    @pl.when((j == 0) & (z > 0))
    def _():
        start(downs)

    x_copy = copy(data.at[own, :], data.at[own, :], s_x, r_x, tm=k ^ 1)
    x_copy.start()

    mine = pl.ds(pl.multiple_of(half * j, half), half)
    forwards, landed = [], []
    for way, put in ((0, 0), (1, 5 * pad)):
        block = data.at[pl.ds(put, pad), mine]
        forwards.append(copy(block, block, s_fwd.at[way], r_fwd.at[way], tm=k ^ 1))
        landed.append(copy(block, block, s_halo.at[0], r_halo.at[way], tm=k ^ 1))

    for cp in sum_copies:
        cp.wait_recv()
    total = sums[0]
    for r in range(1, 8):
        total = total + sums[r]
    mean_ref[...] = total / jnp.full((1, 1), length, jnp.int32).astype(jnp.float32)

    def block(r):
        return pl.ds(pl.multiple_of(rows * (c ^ r), rows), rows)

    def split(w, r, outs, out):
        to_hi, to_lo, to_hi_t, to_lo_t = outs
        h = w.astype(jnp.bfloat16)
        e = (w - h.astype(jnp.float32)).astype(jnp.bfloat16)
        to_hi[out, block(r)] = h
        to_lo[out, block(r)] = e
        h_t, e_t = h.T, e.T
        for u in range(2):
            to = slice(4 * part * u + part * r, 4 * part * u + part * (r + 1))
            to_hi_t[to, out] = h_t[part * u : part * (u + 1)]
            to_lo_t[to, out] = e_t[part * u : part * (u + 1)]

    def windows(when, count, begin, span, outs, at_row):
        t = 2 * steps * z + when + lax.broadcasted_iota(jnp.int32, (count, 1), 0)
        row = 2 * steps * z + when + lax.broadcasted_iota(jnp.int32, (count, span), 0)
        col = 2 * steps * z + begin - pad + lax.broadcasted_iota(jnp.int32, (count, span), 1)
        inside = (col > row - LAG) & (col <= row) & (col >= 0) & (col < length)
        band = inside.astype(jnp.float32).astype(jnp.bfloat16)
        number = jnp.maximum(
            jnp.minimum(t + 1, length) - jnp.maximum(t - (LAG - 1), 0), 0
        ).astype(jnp.float32)
        for r in range(4):
            w = dot(band, data[begin : begin + span, block(r)]) - number * mean_ref[:, block(r)]
            split(w, r, outs, slice(at_row, at_row + count))

    def forward():
        @pl.when(z > 0)
        def _():
            landed[0].wait_recv()
            forwards[0].start()

        @pl.when(z < 3)
        def _():
            landed[1].wait_recv()
            forwards[1].start()

    def triple(u, p, a_hi, a_lo, a_hi_t, a_lo_t):
        at = pl.ds(pl.multiple_of(half * j + 2 * cols * p, 2 * cols), 2 * cols)
        left = slice(4 * part * u, 4 * part * (u + 1))
        return (
            dot(a_hi_t[left, :], a_lo[:, at])
            + dot(a_lo_t[left, :], a_hi[:, at])
            + dot(a_hi_t[left, :], a_hi[:, at])
        )

    before = (hi_e, lo_e, hi_et, lo_et)
    after = (hi, lo, hi_t, lo_t)

    def early_products(u, p):
        ext[u, p] = triple(u, p, *before)

    x_copy.wait_recv()

    @pl.when(z == 0)
    def _():
        windows(0, pad, pad, pad, before, 0)

    @pl.when(z != 0)
    def _():
        for ref in (hi_e, lo_e):
            ref[0:pad, :] = jnp.zeros((pad, width), ref.dtype)
        for ref in (hi_et, lo_et):
            ref[:, 0:pad] = jnp.zeros((width, pad), ref.dtype)

    windows(steps, steps, pad, 2 * steps, before, pad)
    pl.when(j == 0)(forward)
    early_products(0, 0)
    early_products(0, 1)
    early_products(1, 0)
    early_products(1, 1)
    pl.when(j == 1)(forward)

    @pl.when(z > 0)
    def _():
        forwards[0].wait_recv()

    windows(pad, pad, 0, 3 * pad, after, 0)

    @pl.when(z < 3)
    def _():
        forwards[1].wait_recv()

    windows(2 * steps, pad, 3 * pad, 3 * pad, after, pad)

    def send(codes, scales, to_codes, to_scales, sems, **where):
        (sc, rc), (ss, rs) = sems
        return [
            copy(codes, to_codes, sc, rc, **where),
            copy(scales, to_scales, ss, rs, **where),
        ]

    def pack(v, code, scale):
        top = jnp.maximum(jnp.max(jnp.abs(v), axis=0, keepdims=True), 1e-33)
        scale[...] = top * (1.0 / TOP)
        code[...] = jnp.round(v * (TOP / top)).astype(jnp.int32).astype(jnp.int16)

    def unpack(code, scale):
        return code[...].astype(jnp.int32).astype(jnp.float32) * scale[...]

    groups = part // orows

    def group(g):
        return slice(orows * g, orows * (g + 1))

    first_hop, second_hop = [], []
    for m in range(2 * NQ):
        m1 = 1 + m % 2
        first_hop.append([
            send(
                code1.at[m, i], scale1.at[m, i], got1.at[m, i], gots1.at[m, i],
                ((s1.at[m, i], r1.at[m, i]), (s1s.at[m, i], r1s.at[m, i])), chain=c ^ m1,
            )
            for i in range(2)
        ])
        second_hop.append(
            send(
                code2.at[m], scale2.at[m], got2.at[m], gots2.at[m],
                ((s2.at[m], r2.at[m]), (s2s.at[m], r2s.at[m])), chain=c ^ (3 - m1),
            )
        )

    def z_send(n, g):
        to = 4 * (n // 2) + g
        i = jnp.maximum((k ^ to) - 1, 0)
        return send(
            code3.at[n, pl.ds(orows * g, orows), :], scale3.at[n, g], got3.at[n % 2, i],
            gots3.at[n % 2, i],
            ((s3.at[n, g], r3.at[n % 2, i]), (s3s.at[n, g], r3s.at[n % 2, i])), tm=to,
        )

    def z_landed(p, i):
        return send(
            code3.at[p, pl.ds(0, orows), :], scale3.at[p, 0], got3.at[p, i - 1],
            gots3.at[p, i - 1],
            ((s3.at[p, 0], r3.at[p, i - 1]), (s3s.at[p, 0], r3s.at[p, i - 1])), tm=k ^ i,
        )

    def hop2(n):
        for m in (2 * n, 2 * n + 1):
            arrive(first_hop[m][1])
            for g in range(groups):
                v = keep[m, 1, group(g)] + unpack(got1.at[m, 1, group(g)], gots1.at[m, 1, g])
                pack(v, code2.at[m, group(g)], scale2.at[m, g])
            start(second_hop[m])

    def hop3(n):
        for b in range(2):
            m = 2 * n + b
            at = slice(cols * b, cols * (b + 1))
            arrive(first_hop[m][0])
            arrive(second_hop[m])
            for g in range(groups):
                v = (
                    keep[m, 0, group(g)]
                    + unpack(got1.at[m, 0, group(g)], gots1.at[m, 0, g])
                    + unpack(got2.at[m, group(g)], gots2.at[m, g])
                )
                plane[n, group(g), at] = v
                pack(v, code3.at[n, group(g), at], scale3.at[n, g, :, at])
        for g in range(groups):
            @pl.when(k != 4 * (n // 2) + g)
            def _():
                start(z_send(n, g))

    def hop4(p):
        here = plane[2 * (k // 4) + p, pl.ds(pl.multiple_of(orows * (k % 4), orows), orows), :]
        there = None
        for i in (2, 4, 6, 1, 3, 5, 7):
            arrive(z_landed(p, i))
            v = unpack(got3.at[p, i - 1], gots3.at[p, i - 1])
            if i % 2 == 0:
                here = here + v
            else:
                there = v if there is None else there + v
        wide = 2 * cols
        o_ref[:, pl.ds(pl.multiple_of(half * j + wide * p, wide), wide)] = here * scale
        o_ref[:, pl.ds(pl.multiple_of(half * (1 - j) + wide * p, wide), wide)] = there * scale

    def products(n, go):
        u, p = n // 2, n % 2
        w = triple(u, p, hi, lo, hi_t, lo_t) + ext[u, p]
        for r in (3, 1, 2, 0):
            for b in range(2):
                m = 2 * n + b
                v = w[part * r : part * (r + 1), cols * b : cols * (b + 1)]
                if r == 3 or r == 1 + b:
                    slot = int(r == 3)
                    for g in range(groups):
                        pack(v[group(g)], code1.at[m, slot, group(g)], scale1.at[m, slot, g])
                    if slot in go:
                        start(first_hop[m][slot])
                else:
                    keep[m, int(r != 0)] = v

    def first(n, *slots):
        for slot in slots:
            for b in range(2):
                start(first_hop[2 * n + b][slot])

    products(0, (0, 1))
    products(1, (0, 1))
    products(2, (1,))
    products(3, ())
    hop2(0)
    first(2, 0)
    hop2(1)
    first(3, 1, 0)
    hop2(2)
    hop3(0)
    hop3(1)
    hop2(3)
    hop3(2)
    hop3(3)
    hop4(0)
    hop4(1)
    for cp in sum_copies:
        cp.wait_send()
    x_copy.wait_send()

    @pl.when((j == 1) & (z < 3))
    def _():
        for cp in ups:
            cp.wait_send()

    @pl.when((j == 0) & (z > 0))
    def _():
        for cp in downs:
            cp.wait_send()

    @pl.when(z > 0)
    def _():
        forwards[0].wait_send()

    @pl.when(z < 3)
    def _():
        forwards[1].wait_send()

    for m in range(2 * NQ):
        for copies in (*first_hop[m], second_hop[m]):
            for cp in copies:
                cp.wait_send()
    for n in range(NQ):
        for g in range(groups):
            @pl.when(k != 4 * (n // 2) + g)
            def _():
                for cp in z_send(n, g):
                    cp.wait_send()


def hbm(x):
    return pltpu.with_memory_space_constraint(x, pltpu.HBM)


def fused(traces, lengths):
    _, steps, width = traces.shape
    f32, bf16, i16 = jnp.float32, jnp.bfloat16, jnp.int16
    rows, cols = width // 4, width // 2 // NQ
    part, groups = rows // 2, 4
    dma = pltpu.SemaphoreType.DMA
    return pl.pallas_call(
        kernel,
        out_shape=jax.ShapeDtypeStruct((width // 32, width), f32),
        in_specs=[
            pl.BlockSpec(memory_space=pltpu.HBM),
            pl.BlockSpec(memory_space=pltpu.HBM),
        ],
        out_specs=pl.BlockSpec(memory_space=pltpu.VMEM),
        scratch_shapes=[
            pltpu.SMEM(lengths.shape, jnp.int32),
            pltpu.VMEM((3 * steps, width), bf16),
            pltpu.VMEM((2, NQ // 2, 2 * rows, 2 * cols), f32),
            pltpu.VMEM((3 * steps // 2, width), bf16),
            pltpu.VMEM((3 * steps // 2, width), bf16),
            pltpu.VMEM((width, 3 * steps // 2), bf16),
            pltpu.VMEM((width, 3 * steps // 2), bf16),
            pltpu.VMEM((8, 1, width), f32),
            pltpu.VMEM((steps, width), bf16),
            pltpu.VMEM((steps, width), bf16),
            pltpu.VMEM((width, steps), bf16),
            pltpu.VMEM((width, steps), bf16),
            pltpu.VMEM((2 * NQ, 2, part, cols), f32),
            pltpu.VMEM((2 * NQ, 2, part, cols), i16),
            pltpu.VMEM((2 * NQ, 2, groups, 1, cols), f32),
            pltpu.VMEM((2 * NQ, 2, part, cols), i16),
            pltpu.VMEM((2 * NQ, 2, groups, 1, cols), f32),
            pltpu.VMEM((2 * NQ, part, cols), i16),
            pltpu.VMEM((2 * NQ, groups, 1, cols), f32),
            pltpu.VMEM((2 * NQ, part, cols), i16),
            pltpu.VMEM((2 * NQ, groups, 1, cols), f32),
            pltpu.VMEM((NQ, part, 2 * cols), f32),
            pltpu.VMEM((NQ, part, 2 * cols), i16),
            pltpu.VMEM((NQ, groups, 1, 2 * cols), f32),
            pltpu.VMEM((2, 7, rows // 8, 2 * cols), i16),
            pltpu.VMEM((2, 7, 1, 2 * cols), f32),
            pltpu.VMEM((1, width), f32),
            dma((2,)),
            dma((8,)), dma((8,)),
            dma, dma,
            dma((2,)), dma((2,)),
            dma((2,)), dma((2,)),
            dma((2 * NQ, 2)), dma((2 * NQ, 2)), dma((2 * NQ, 2)), dma((2 * NQ, 2)),
            dma((2 * NQ,)), dma((2 * NQ,)), dma((2 * NQ,)), dma((2 * NQ,)),
            dma((NQ, 4)), dma((2, 7)), dma((NQ, 4)), dma((2, 7)),
        ],
        compiler_params=pltpu.CompilerParams(
            collective_id=0, has_side_effects=True, vmem_limit_bytes=24 * 2**20
        ),
    )(hbm(lengths), hbm(traces.reshape(steps, width)))


def body(mesh, traces, lengths):
    chains, steps, width = traces.shape
    laid_out = (
        mesh.shape["groups"] == 1 and mesh.shape["chain"] == 4 and mesh.shape["tm"] == 8
    )
    if laid_out and chains == 1 and steps == LAG and width == 1024:
        return fused(traces, lengths)
    return on_device(traces, lengths)


def solution(mesh):
    in_specs = (P(("groups", "chain"), "tm", None), P("groups"))
    out_specs = P(("groups", "chain", "tm"), None)
    return jax.shard_map(
        functools.partial(body, mesh), mesh=mesh, in_specs=in_specs, out_specs=out_specs,
        check_vma=False,
    )
```

```python
import functools

import jax
import jax.numpy as jnp
from jax import lax
from jax.experimental import pallas as pl
from jax.experimental.pallas import tpu as pltpu
from jax.sharding import PartitionSpec as P

LAG = 256
MESH = pl.DeviceIdType.MESH


def shifted(block, axis, distance):
    devices = range(lax.axis_size(axis))
    route = [(i - distance, i) for i in devices if i - distance in devices]
    return lax.ppermute(block, axis, route)


def window_sums(current, previous):
    chains, steps, width = current.shape
    count = steps // LAG
    blocks = current.reshape(chains, count, LAG, width)
    earlier = jnp.concatenate([previous[:, None], blocks[:, :-1]], axis=1)
    index = jnp.arange(LAG)
    lower = index[None, :] <= index[:, None]
    upper = index[None, :] > index[:, None]
    lower_mat = lower.astype(jnp.float32)
    upper_mat = upper.astype(jnp.float32)
    result = jnp.einsum("ij,cbjp->cbip", lower_mat, blocks, precision=lax.Precision.HIGHEST)
    result = result + jnp.einsum(
        "ij,cbjp->cbip", upper_mat, earlier, precision=lax.Precision.HIGHEST
    )
    return result.reshape(chains, steps, width)


def gram_rows(filtered):
    chains, steps, width = filtered.shape
    flat = filtered.reshape(chains * steps, width)
    return jnp.einsum("tk,tp->kp", flat, flat, precision=lax.Precision.HIGHEST)


def on_device(traces, lengths):
    chains, steps, width = traces.shape
    own_len = lax.dynamic_slice_in_dim(lengths, lax.axis_index("chain") * chains, chains)
    first_time = lax.axis_index("tm") * steps
    times = first_time + jnp.arange(steps, dtype=jnp.int32)
    valid = (times[None, :] < own_len[:, None]).astype(jnp.float32)
    back_times = times - steps
    back_valid = ((back_times[None, :] >= 0) & (back_times[None, :] < own_len[:, None])).astype(
        jnp.float32
    )
    behind = shifted(traces, "tm", 1)
    data = traces.astype(jnp.float32) * valid[..., None]
    earlier = behind.astype(jnp.float32) * back_valid[..., None]
    totals = lax.psum(jnp.sum(data, axis=1), "tm")
    mean = totals / own_len.astype(jnp.float32)[:, None]
    scale = 1.0 / (LAG * jnp.sum(lengths).astype(jnp.float32))
    centered = window_sums(
        (data - mean[:, None, :]) * valid[..., None],
        (earlier - mean[:, None, :]) * back_valid[..., None],
    )
    return lax.psum_scatter(
        scale * gram_rows(centered), ("chain", "tm"), scatter_dimension=0, tiled=True
    )


def dot(a, b):
    return jnp.dot(a, b, preferred_element_type=jnp.float32)


NQ = 4
TOP = 32767.0


def kernel(
    len_hbm, x_hbm, o_ref, len_ref, data, ext, hi_e, lo_e, hi_et, lo_et, sums, hi, lo, hi_t, lo_t, keep, code1, scale1, got1,
    gots1, code2, scale2, got2, gots2, plane, code3, scale3, got3, gots3, mean_ref, band_first, band_own, band_low, band_high, in_sem, s_sum, r_sum, s_x, r_x,
    s_halo, r_halo, s_fwd, r_fwd, s1, r1, s1s,
    r1s, s2, r2, s2s, r2s, s3, r3, s3s, r3s,
):
    steps, width = x_hbm.shape
    pad = steps // 2
    half = width // 2
    cols = half // NQ
    rows = width // 4
    part = rows // 2
    orows = rows // 8
    c = lax.axis_index("chain")
    k = lax.axis_index("tm")
    z = k // 2
    j = k % 2

    def copy(src, dst, send, recv, **where):
        return pltpu.make_async_remote_copy(
            src_ref=src, dst_ref=dst, send_sem=send, recv_sem=recv, device_id=where,
            device_id_type=MESH,
        )

    def start(copies):
        for cp in copies:
            cp.start()

    def arrive(copies):
        for cp in copies:
            cp.wait_recv()

    own = pl.ds(pl.multiple_of(pad + steps * j, pad), steps)
    len_in = pltpu.make_async_copy(len_hbm, len_ref, in_sem.at[0])
    x_in = pltpu.make_async_copy(x_hbm, data.at[own, :], in_sem.at[1])
    len_in.start()
    x_in.start()
    barrier = pltpu.get_barrier_semaphore()
    for r in range(1, 8):
        pl.semaphore_signal(barrier, inc=1, device_id={"tm": k ^ r}, device_id_type=MESH)
    for r in (1, 2):
        pl.semaphore_signal(barrier, inc=1, device_id={"chain": c ^ r}, device_id_type=MESH)

    len_in.wait()
    length = len_ref[c]
    total_len = len_ref[0]
    for i in range(1, len_ref.shape[0]):
        total_len = total_len + len_ref[i]
    scale = 1.0 / (LAG * jnp.full((1, 1), total_len, jnp.int32).astype(jnp.float32))

    time = k * steps + lax.broadcasted_iota(jnp.int32, (steps, 1), 0)
    valid = (time < length).astype(jnp.float32)
    x_in.wait()
    sums[0] = jnp.sum(data[own, :].astype(jnp.float32) * valid, axis=0, keepdims=True)

    @pl.when(z == 0)
    def _():
        data[0:pad, :] = jnp.zeros((pad, width), data.dtype)

    @pl.when(z != 0)
    def _():
        for ref in (hi_e, lo_e):
            ref[0:pad, :] = jnp.zeros((pad, width), ref.dtype)
        for ref in (hi_et, lo_et):
            ref[:, 0:pad] = jnp.zeros((width, pad), ref.dtype)

    @pl.when(z == 3)
    def _():
        data[5 * pad : 6 * pad, :] = jnp.zeros((pad, width), data.dtype)

    pl.semaphore_wait(barrier, 9)

    sum_copies = [
        copy(sums.at[0], sums.at[r], s_sum.at[r], r_sum.at[r], tm=k ^ r) for r in range(1, 8)
    ]
    for cp in sum_copies:
        cp.start()
    def halo(way, h):
        near = 2 * jnp.minimum(z + 1, 3) if way == 0 else 2 * jnp.maximum(z - 1, 0)
        take = 4 * pad if way == 0 else pad
        put = 0 if way == 0 else 5 * pad
        at = pl.ds(half * h, half)
        return copy(
            data.at[pl.ds(take, pad), at], data.at[pl.ds(put, pad), at], s_halo.at[h],
            r_halo.at[way], tm=near + h,
        )

    ups = [halo(0, h) for h in range(2)]
    downs = [halo(1, h) for h in range(2)]

    @pl.when((j == 1) & (z < 3))
    def _():
        start(ups)

    @pl.when((j == 0) & (z > 0))
    def _():
        start(downs)

    x_copy = copy(data.at[own, :], data.at[own, :], s_x, r_x, tm=k ^ 1)
    x_copy.start()

    mine = pl.ds(pl.multiple_of(half * j, half), half)
    forwards, landed = [], []
    for way, put in ((0, 0), (1, 5 * pad)):
        block = data.at[pl.ds(put, pad), mine]
        forwards.append(copy(block, block, s_fwd.at[way], r_fwd.at[way], tm=k ^ 1))
        landed.append(copy(block, block, s_halo.at[0], r_halo.at[way], tm=k ^ 1))

    def set_band(band, when, begin):
        row = 2 * steps * z + when + lax.broadcasted_iota(jnp.int32, band.shape, 0)
        col = 2 * steps * z + begin - pad + lax.broadcasted_iota(jnp.int32, band.shape, 1)
        inside = (col > row - LAG) & (col <= row) & (col >= 0) & (col < length)
        band[...] = inside.astype(jnp.float32).astype(jnp.bfloat16)

    set_band(band_first, 0, pad)
    set_band(band_own, steps, pad)
    set_band(band_low, pad, 0)
    set_band(band_high, 2 * steps, 3 * pad)
    for cp in sum_copies:
        cp.wait_recv()
    total = sums[0]
    for r in range(1, 8):
        total = total + sums[r]
    mean_ref[...] = total / jnp.full((1, 1), length, jnp.int32).astype(jnp.float32)

    def split(w, b, outs, out):
        to_hi, to_lo, to_hi_t, to_lo_t = outs
        at = slice(rows * b, rows * (b + 1))
        h = w.astype(jnp.bfloat16)
        e = (w - h.astype(jnp.float32)).astype(jnp.bfloat16)
        to_hi[out, at] = h
        to_lo[out, at] = e
        h_t, e_t = h.T, e.T
        for u in range(2):
            to = pl.ds(pl.multiple_of(4 * part * u + part * (c ^ b), part), part)
            to_hi_t[to, out] = h_t[part * u : part * (u + 1)]
            to_lo_t[to, out] = e_t[part * u : part * (u + 1)]

    def windows(when, count, begin, span, band, outs, at_row, blocks=(0, 1, 2, 3)):
        t = 2 * steps * z + when + lax.broadcasted_iota(jnp.int32, (count, 1), 0)
        number = jnp.maximum(
            jnp.minimum(t + 1, length) - jnp.maximum(t - (LAG - 1), 0), 0
        ).astype(jnp.float32)
        for b in blocks:
            at = slice(rows * b, rows * (b + 1))
            w = dot(band[...], data[begin : begin + span, at]) - number * mean_ref[:, at]
            split(w, b, outs, slice(at_row, at_row + count))

    def forward():
        @pl.when(z > 0)
        def _():
            landed[0].wait_recv()
            forwards[0].start()

        @pl.when(z < 3)
        def _():
            landed[1].wait_recv()
            forwards[1].start()

    def triple(u, p, a_hi, a_lo, a_hi_t, a_lo_t):
        at = pl.ds(pl.multiple_of(half * j + 2 * cols * p, 2 * cols), 2 * cols)
        left = slice(4 * part * u, 4 * part * (u + 1))
        return (
            dot(a_hi_t[left, :], a_lo[:, at])
            + dot(a_lo_t[left, :], a_hi[:, at])
            + dot(a_hi_t[left, :], a_hi[:, at])
        )

    before = (hi_e, lo_e, hi_et, lo_et)
    after = (hi, lo, hi_t, lo_t)

    def early_products(u, p):
        ext[u, p] = triple(u, p, *before)

    x_copy.wait_recv()

    @pl.when(z == 0)
    def _():
        windows(0, pad, pad, pad, band_first, before, 0)

    windows(steps, steps, pad, 2 * steps, band_own, before, pad)
    pl.when(j == 0)(forward)
    early_products(0, 0)
    early_products(0, 1)
    early_products(1, 0)
    early_products(1, 1)
    pl.when(j == 1)(forward)

    @pl.when(z > 0)
    def _():
        forwards[0].wait_recv()

    windows(pad, pad, 0, 3 * pad, band_low, after, 0)

    @pl.when(z < 3)
    def _():
        forwards[1].wait_recv()

    windows(2 * steps, pad, 3 * pad, 3 * pad, band_high, after, pad)

    def send(codes, scales, to_codes, to_scales, sems, **where):
        (sc, rc), (ss, rs) = sems
        return [
            copy(codes, to_codes, sc, rc, **where),
            copy(scales, to_scales, ss, rs, **where),
        ]

    def pack(v, code, scale):
        top = jnp.maximum(jnp.max(jnp.abs(v), axis=0, keepdims=True), 1e-33)
        scale[...] = top * (1.0 / TOP)
        code[...] = jnp.round(v * (TOP / top)).astype(jnp.int32).astype(jnp.int16)

    def unpack(code, scale):
        return code[...].astype(jnp.int32).astype(jnp.float32) * scale[...]

    groups = part // orows

    def group(g):
        return slice(orows * g, orows * (g + 1))

    first_hop, second_hop = [], []
    for m in range(2 * NQ):
        m1 = 1 + m % 2
        first_hop.append([
            send(
                code1.at[m, i], scale1.at[m, i], got1.at[m, i], gots1.at[m, i],
                ((s1.at[m, i], r1.at[m, i]), (s1s.at[m, i], r1s.at[m, i])), chain=c ^ m1,
            )
            for i in range(2)
        ])
        second_hop.append(
            send(
                code2.at[m], scale2.at[m], got2.at[m], gots2.at[m],
                ((s2.at[m], r2.at[m]), (s2s.at[m], r2s.at[m])), chain=c ^ (3 - m1),
            )
        )

    def z_send(n, g):
        to = 4 * (n // 2) + g
        i = jnp.maximum((k ^ to) - 1, 0)
        return send(
            code3.at[n, pl.ds(orows * g, orows), :], scale3.at[n, g], got3.at[n % 2, i],
            gots3.at[n % 2, i],
            ((s3.at[n, g], r3.at[n % 2, i]), (s3s.at[n, g], r3s.at[n % 2, i])), tm=to,
        )

    def z_landed(p, i):
        return send(
            code3.at[p, pl.ds(0, orows), :], scale3.at[p, 0], got3.at[p, i - 1],
            gots3.at[p, i - 1],
            ((s3.at[p, 0], r3.at[p, i - 1]), (s3s.at[p, 0], r3s.at[p, i - 1])), tm=k ^ i,
        )

    def hop2(n):
        for m in (2 * n, 2 * n + 1):
            arrive(first_hop[m][1])
            for g in range(groups):
                v = keep[m, 1, group(g)] + unpack(got1.at[m, 1, group(g)], gots1.at[m, 1, g])
                pack(v, code2.at[m, group(g)], scale2.at[m, g])
            start(second_hop[m])

    def hop3(n):
        for b in range(2):
            m = 2 * n + b
            at = slice(cols * b, cols * (b + 1))
            arrive(first_hop[m][0])
            arrive(second_hop[m])
            for g in range(groups):
                v = (
                    keep[m, 0, group(g)]
                    + unpack(got1.at[m, 0, group(g)], gots1.at[m, 0, g])
                    + unpack(got2.at[m, group(g)], gots2.at[m, g])
                )
                plane[n, group(g), at] = v
                pack(v, code3.at[n, group(g), at], scale3.at[n, g, :, at])
    def spread(n, *targets):
        for g in targets:
            @pl.when(k != 4 * (n // 2) + g)
            def _():
                start(z_send(n, g))

    def hop4(p):
        here = plane[2 * (k // 4) + p, pl.ds(pl.multiple_of(orows * (k % 4), orows), orows), :]
        there = None
        for i in (2, 4, 6, 1, 3, 5, 7):
            arrive(z_landed(p, i))
            v = unpack(got3.at[p, i - 1], gots3.at[p, i - 1])
            if i % 2 == 0:
                here = here + v
            else:
                there = v if there is None else there + v
        wide = 2 * cols
        o_ref[:, pl.ds(pl.multiple_of(half * j + wide * p, wide), wide)] = here * scale
        o_ref[:, pl.ds(pl.multiple_of(half * (1 - j) + wide * p, wide), wide)] = there * scale

    def products(n, go):
        u, p = n // 2, n % 2
        w = triple(u, p, hi, lo, hi_t, lo_t) + ext[u, p]
        for r in (3, 1, 2, 0):
            for b in range(2):
                m = 2 * n + b
                v = w[part * r : part * (r + 1), cols * b : cols * (b + 1)]
                if r == 3 or r == 1 + b:
                    slot = int(r == 3)
                    for g in range(groups):
                        pack(v[group(g)], code1.at[m, slot, group(g)], scale1.at[m, slot, g])
                    if slot in go:
                        start(first_hop[m][slot])
                else:
                    keep[m, int(r != 0)] = v

    def first(n, *slots):
        for slot in slots:
            for b in range(2):
                start(first_hop[2 * n + b][slot])

    products(0, (0, 1))
    products(1, (0, 1))
    products(2, (1,))
    products(3, (1,))
    hop2(0)
    hop2(1)
    first(2, 0)
    hop2(2)
    first(3, 0)
    hop2(3)
    hop3(0)
    spread(0, 0, 1)
    hop3(1)
    spread(1, 0, 1)
    spread(0, 2, 3)
    spread(1, 2, 3)
    hop3(2)
    spread(2, 0, 1, 2, 3)
    hop3(3)
    spread(3, 0, 1, 2, 3)
    for cp in sum_copies:
        cp.wait_send()
    x_copy.wait_send()

    @pl.when((j == 1) & (z < 3))
    def _():
        for cp in ups:
            cp.wait_send()

    @pl.when((j == 0) & (z > 0))
    def _():
        for cp in downs:
            cp.wait_send()

    @pl.when(z > 0)
    def _():
        forwards[0].wait_send()

    @pl.when(z < 3)
    def _():
        forwards[1].wait_send()

    for m in range(2 * NQ):
        for copies in (*first_hop[m], second_hop[m]):
            for cp in copies:
                cp.wait_send()
    hop4(0)
    hop4(1)
    for n in range(NQ):
        for g in range(groups):
            @pl.when(k != 4 * (n // 2) + g)
            def _():
                for cp in z_send(n, g):
                    cp.wait_send()


def hbm(x):
    return pltpu.with_memory_space_constraint(x, pltpu.HBM)


def fused(traces, lengths):
    _, steps, width = traces.shape
    f32, bf16, i16 = jnp.float32, jnp.bfloat16, jnp.int16
    rows, cols = width // 4, width // 2 // NQ
    part, groups = rows // 2, 4
    dma = pltpu.SemaphoreType.DMA
    return pl.pallas_call(
        kernel,
        out_shape=jax.ShapeDtypeStruct((width // 32, width), f32),
        in_specs=[
            pl.BlockSpec(memory_space=pltpu.HBM),
            pl.BlockSpec(memory_space=pltpu.HBM),
        ],
        out_specs=pl.BlockSpec(memory_space=pltpu.VMEM),
        scratch_shapes=[
            pltpu.SMEM(lengths.shape, jnp.int32),
            pltpu.VMEM((3 * steps, width), bf16),
            pltpu.VMEM((2, NQ // 2, 2 * rows, 2 * cols), f32),
            pltpu.VMEM((3 * steps // 2, width), bf16),
            pltpu.VMEM((3 * steps // 2, width), bf16),
            pltpu.VMEM((width, 3 * steps // 2), bf16),
            pltpu.VMEM((width, 3 * steps // 2), bf16),
            pltpu.VMEM((8, 1, width), f32),
            pltpu.VMEM((steps, width), bf16),
            pltpu.VMEM((steps, width), bf16),
            pltpu.VMEM((width, steps), bf16),
            pltpu.VMEM((width, steps), bf16),
            pltpu.VMEM((2 * NQ, 2, part, cols), f32),
            pltpu.VMEM((2 * NQ, 2, part, cols), i16),
            pltpu.VMEM((2 * NQ, 2, groups, 1, cols), f32),
            pltpu.VMEM((2 * NQ, 2, part, cols), i16),
            pltpu.VMEM((2 * NQ, 2, groups, 1, cols), f32),
            pltpu.VMEM((2 * NQ, part, cols), i16),
            pltpu.VMEM((2 * NQ, groups, 1, cols), f32),
            pltpu.VMEM((2 * NQ, part, cols), i16),
            pltpu.VMEM((2 * NQ, groups, 1, cols), f32),
            pltpu.VMEM((NQ, part, 2 * cols), f32),
            pltpu.VMEM((NQ, part, 2 * cols), i16),
            pltpu.VMEM((NQ, groups, 1, 2 * cols), f32),
            pltpu.VMEM((2, 7, rows // 8, 2 * cols), i16),
            pltpu.VMEM((2, 7, 1, 2 * cols), f32),
            pltpu.VMEM((1, width), f32),
            pltpu.VMEM((steps // 2, steps // 2), bf16),
            pltpu.VMEM((steps, 2 * steps), bf16),
            pltpu.VMEM((steps // 2, 3 * steps // 2), bf16),
            pltpu.VMEM((steps // 2, 3 * steps // 2), bf16),
            dma((2,)),
            dma((8,)), dma((8,)),
            dma, dma,
            dma((2,)), dma((2,)),
            dma((2,)), dma((2,)),
            dma((2 * NQ, 2)), dma((2 * NQ, 2)), dma((2 * NQ, 2)), dma((2 * NQ, 2)),
            dma((2 * NQ,)), dma((2 * NQ,)), dma((2 * NQ,)), dma((2 * NQ,)),
            dma((NQ, 4)), dma((2, 7)), dma((NQ, 4)), dma((2, 7)),
        ],
        compiler_params=pltpu.CompilerParams(
            collective_id=0, has_side_effects=True, vmem_limit_bytes=24 * 2**20
        ),
    )(hbm(lengths), hbm(traces.reshape(steps, width)))


def body(mesh, traces, lengths):
    chains, steps, width = traces.shape
    laid_out = (
        mesh.shape["groups"] == 1 and mesh.shape["chain"] == 4 and mesh.shape["tm"] == 8
    )
    if laid_out and chains == 1 and steps == LAG and width == 1024:
        return fused(traces, lengths)
    return on_device(traces, lengths)


def solution(mesh):
    in_specs = (P(("groups", "chain"), "tm", None), P("groups"))
    out_specs = P(("groups", "chain", "tm"), None)
    return jax.shard_map(
        functools.partial(body, mesh), mesh=mesh, in_specs=in_specs, out_specs=out_specs,
        check_vma=False,
    )
```

```python
import functools

import jax
import jax.numpy as jnp
from jax import lax
from jax.experimental import pallas as pl
from jax.experimental.pallas import tpu as pltpu
from jax.sharding import PartitionSpec as P

LAG = 256
MESH = pl.DeviceIdType.MESH


def shifted(block, axis, distance):
    devices = range(lax.axis_size(axis))
    route = [(i - distance, i) for i in devices if i - distance in devices]
    return lax.ppermute(block, axis, route)


def window_sums(current, previous):
    chains, steps, width = current.shape
    count = steps // LAG
    blocks = current.reshape(chains, count, LAG, width)
    earlier = jnp.concatenate([previous[:, None], blocks[:, :-1]], axis=1)
    index = jnp.arange(LAG)
    lower = index[None, :] <= index[:, None]
    upper = index[None, :] > index[:, None]
    lower_mat = lower.astype(jnp.float32)
    upper_mat = upper.astype(jnp.float32)
    result = jnp.einsum("ij,cbjp->cbip", lower_mat, blocks, precision=lax.Precision.HIGHEST)
    result = result + jnp.einsum(
        "ij,cbjp->cbip", upper_mat, earlier, precision=lax.Precision.HIGHEST
    )
    return result.reshape(chains, steps, width)


def gram_rows(filtered):
    chains, steps, width = filtered.shape
    flat = filtered.reshape(chains * steps, width)
    return jnp.einsum("tk,tp->kp", flat, flat, precision=lax.Precision.HIGHEST)


def on_device(traces, lengths):
    chains, steps, width = traces.shape
    own_len = lax.dynamic_slice_in_dim(lengths, lax.axis_index("chain") * chains, chains)
    first_time = lax.axis_index("tm") * steps
    times = first_time + jnp.arange(steps, dtype=jnp.int32)
    valid = (times[None, :] < own_len[:, None]).astype(jnp.float32)
    back_times = times - steps
    back_valid = ((back_times[None, :] >= 0) & (back_times[None, :] < own_len[:, None])).astype(
        jnp.float32
    )
    behind = shifted(traces, "tm", 1)
    data = traces.astype(jnp.float32) * valid[..., None]
    earlier = behind.astype(jnp.float32) * back_valid[..., None]
    totals = lax.psum(jnp.sum(data, axis=1), "tm")
    mean = totals / own_len.astype(jnp.float32)[:, None]
    scale = 1.0 / (LAG * jnp.sum(lengths).astype(jnp.float32))
    centered = window_sums(
        (data - mean[:, None, :]) * valid[..., None],
        (earlier - mean[:, None, :]) * back_valid[..., None],
    )
    return lax.psum_scatter(
        scale * gram_rows(centered), ("chain", "tm"), scatter_dimension=0, tiled=True
    )


def dot(a, b):
    return jnp.dot(a, b, preferred_element_type=jnp.float32)


NQ = 4
TOP = 32767.0


def kernel(
    len_hbm, x_hbm, o_ref, len_ref, data, ext, hi_e, lo_e, hi_et, lo_et, sums, hi, lo, hi_t, lo_t, keep, code1, scale1, got1,
    gots1, code2, scale2, got2, gots2, plane, code3, scale3, got3, gots3, mean_ref, band_first, band_own, band_low, band_high, in_sem, s_sum, r_sum, s_x, r_x,
    s_halo, r_halo, s_fwd, r_fwd, s1, r1, s1s,
    r1s, s2, r2, s2s, r2s, s3, r3, s3s, r3s,
):
    steps, width = x_hbm.shape
    pad = steps // 2
    half = width // 2
    cols = half // NQ
    rows = width // 4
    part = rows // 2
    orows = rows // 8
    c = lax.axis_index("chain")
    k = lax.axis_index("tm")
    z = k // 2
    j = k % 2

    def copy(src, dst, send, recv, **where):
        return pltpu.make_async_remote_copy(
            src_ref=src, dst_ref=dst, send_sem=send, recv_sem=recv, device_id=where,
            device_id_type=MESH,
        )

    def start(copies):
        for cp in copies:
            cp.start()

    def leave(copies):
        for cp in copies:
            cp.wait_send()

    def arrive(copies):
        for cp in copies:
            cp.wait_recv()

    own = pl.ds(pl.multiple_of(pad + steps * j, pad), steps)
    len_in = pltpu.make_async_copy(len_hbm, len_ref, in_sem.at[0])
    x_in = pltpu.make_async_copy(x_hbm, data.at[own, :], in_sem.at[1])
    len_in.start()
    x_in.start()
    barrier = pltpu.get_barrier_semaphore()
    for r in range(1, 8):
        pl.semaphore_signal(barrier, inc=1, device_id={"tm": k ^ r}, device_id_type=MESH)
    for r in (1, 2):
        pl.semaphore_signal(barrier, inc=1, device_id={"chain": c ^ r}, device_id_type=MESH)

    len_in.wait()
    length = len_ref[c]
    total_len = len_ref[0]
    for i in range(1, len_ref.shape[0]):
        total_len = total_len + len_ref[i]
    scale = 1.0 / (LAG * jnp.full((1, 1), total_len, jnp.int32).astype(jnp.float32))

    time = k * steps + lax.broadcasted_iota(jnp.int32, (steps, 1), 0)
    valid = (time < length).astype(jnp.float32)
    x_in.wait()
    sums[0] = jnp.sum(data[own, :].astype(jnp.float32) * valid, axis=0, keepdims=True)

    @pl.when(z == 0)
    def _():
        data[0:pad, :] = jnp.zeros((pad, width), data.dtype)

    @pl.when(z != 0)
    def _():
        for ref in (hi_e, lo_e):
            ref[0:pad, :] = jnp.zeros((pad, width), ref.dtype)
        for ref in (hi_et, lo_et):
            ref[:, 0:pad] = jnp.zeros((width, pad), ref.dtype)

    @pl.when(z == 3)
    def _():
        data[5 * pad : 6 * pad, :] = jnp.zeros((pad, width), data.dtype)

    pl.semaphore_wait(barrier, 9)

    sum_copies = [
        copy(sums.at[0], sums.at[r], s_sum.at[r], r_sum.at[r], tm=k ^ r) for r in range(1, 8)
    ]
    for cp in sum_copies:
        cp.start()
    def halo(way, h):
        near = 2 * jnp.minimum(z + 1, 3) if way == 0 else 2 * jnp.maximum(z - 1, 0)
        take = 4 * pad if way == 0 else pad
        put = 0 if way == 0 else 5 * pad
        at = pl.ds(half * h, half)
        return copy(
            data.at[pl.ds(take, pad), at], data.at[pl.ds(put, pad), at], s_halo.at[h],
            r_halo.at[way], tm=near + h,
        )

    ups = [halo(0, h) for h in range(2)]
    downs = [halo(1, h) for h in range(2)]

    @pl.when((j == 1) & (z < 3))
    def _():
        start(ups)

    @pl.when((j == 0) & (z > 0))
    def _():
        start(downs)

    x_copy = copy(data.at[own, :], data.at[own, :], s_x, r_x, tm=k ^ 1)
    x_copy.start()

    mine = pl.ds(pl.multiple_of(half * j, half), half)
    forwards, landed = [], []
    for way, put in ((0, 0), (1, 5 * pad)):
        block = data.at[pl.ds(put, pad), mine]
        forwards.append(copy(block, block, s_fwd.at[way], r_fwd.at[way], tm=k ^ 1))
        landed.append(copy(block, block, s_halo.at[0], r_halo.at[way], tm=k ^ 1))

    def set_band(band, when, begin):
        row = 2 * steps * z + when + lax.broadcasted_iota(jnp.int32, band.shape, 0)
        col = 2 * steps * z + begin - pad + lax.broadcasted_iota(jnp.int32, band.shape, 1)
        inside = (col > row - LAG) & (col <= row) & (col >= 0) & (col < length)
        band[...] = inside.astype(jnp.float32).astype(jnp.bfloat16)

    set_band(band_first, 0, pad)
    set_band(band_own, steps, pad)
    set_band(band_low, pad, 0)
    set_band(band_high, 2 * steps, 3 * pad)
    for cp in sum_copies:
        cp.wait_recv()
    total = sums[0]
    for r in range(1, 8):
        total = total + sums[r]
    mean_ref[...] = total / jnp.full((1, 1), length, jnp.int32).astype(jnp.float32)

    def split(w, b, outs, out):
        to_hi, to_lo, to_hi_t, to_lo_t = outs
        at = slice(rows * b, rows * (b + 1))
        h = w.astype(jnp.bfloat16)
        e = (w - h.astype(jnp.float32)).astype(jnp.bfloat16)
        to_hi[out, at] = h
        to_lo[out, at] = e
        h_t, e_t = h.T, e.T
        for u in range(2):
            to = pl.ds(pl.multiple_of(4 * part * u + part * (c ^ b), part), part)
            to_hi_t[to, out] = h_t[part * u : part * (u + 1)]
            to_lo_t[to, out] = e_t[part * u : part * (u + 1)]

    def windows(when, count, begin, span, band, outs, at_row, blocks=(0, 1, 2, 3)):
        t = 2 * steps * z + when + lax.broadcasted_iota(jnp.int32, (count, 1), 0)
        number = jnp.maximum(
            jnp.minimum(t + 1, length) - jnp.maximum(t - (LAG - 1), 0), 0
        ).astype(jnp.float32)
        for b in blocks:
            at = slice(rows * b, rows * (b + 1))
            w = dot(band[...], data[begin : begin + span, at]) - number * mean_ref[:, at]
            split(w, b, outs, slice(at_row, at_row + count))

    def forward():
        @pl.when(z > 0)
        def _():
            landed[0].wait_recv()
            forwards[0].start()

        @pl.when(z < 3)
        def _():
            landed[1].wait_recv()
            forwards[1].start()

    early_side = jnp.where(z == 0, 1, 0)

    def side(turn):
        return 1 - early_side if turn else early_side

    def triple(u, p, a_hi, a_lo, a_hi_t, a_lo_t):
        at = pl.ds(pl.multiple_of(half * j + 2 * cols * p, 2 * cols), 2 * cols)
        left = pl.ds(pl.multiple_of(4 * part * side(u), 4 * part), 4 * part)
        return (
            dot(a_hi_t[left, :], a_lo[:, at])
            + dot(a_lo_t[left, :], a_hi[:, at])
            + dot(a_hi_t[left, :], a_hi[:, at])
        )

    before = (hi_e, lo_e, hi_et, lo_et)
    after = (hi, lo, hi_t, lo_t)

    def early_products(u, p):
        ext[u, p] = triple(u, p, *before)

    x_copy.wait_recv()

    @pl.when(z == 0)
    def _():
        windows(0, pad, pad, pad, band_first, before, 0)

    windows(steps, steps, pad, 2 * steps, band_own, before, pad)
    pl.when(j == 0)(forward)
    early_products(0, 0)
    early_products(0, 1)
    early_products(1, 0)
    early_products(1, 1)
    pl.when(j == 1)(forward)

    @pl.when(z > 0)
    def _():
        forwards[0].wait_recv()

    windows(pad, pad, 0, 3 * pad, band_low, after, 0)

    @pl.when(z < 3)
    def _():
        forwards[1].wait_recv()

    windows(2 * steps, pad, 3 * pad, 3 * pad, band_high, after, pad)

    def send(codes, scales, to_codes, to_scales, sems, **where):
        (sc, rc), (ss, rs) = sems
        return [
            copy(codes, to_codes, sc, rc, **where),
            copy(scales, to_scales, ss, rs, **where),
        ]

    def pack(v, code, scale):
        top = jnp.maximum(jnp.max(jnp.abs(v), axis=0, keepdims=True), 1e-33)
        scale[...] = top * (1.0 / TOP)
        code[...] = jnp.round(v * (TOP / top)).astype(jnp.int32).astype(jnp.int16)

    def unpack(code, scale):
        return code[...].astype(jnp.int32).astype(jnp.float32) * scale[...]

    groups = part // orows

    def group(g):
        return slice(orows * g, orows * (g + 1))

    first_hop, second_hop = [], []
    for m in range(2 * NQ):
        m1 = 1 + m % 2
        first_hop.append([
            send(
                code1.at[m, i], scale1.at[m, i], got1.at[m, i], gots1.at[m, i],
                ((s1.at[m, i], r1.at[m, i]), (s1s.at[m, i], r1s.at[m, i])), chain=c ^ m1,
            )
            for i in range(2)
        ])
        second_hop.append(
            send(
                code2.at[m], scale2.at[m], got2.at[m], gots2.at[m],
                ((s2.at[m], r2.at[m]), (s2s.at[m], r2s.at[m])), chain=c ^ (3 - m1),
            )
        )

    def z_send(n, g):
        to = 4 * side(n // 2) + g
        i = jnp.maximum((k ^ to) - 1, 0)
        return send(
            code3.at[n, pl.ds(orows * g, orows), :], scale3.at[n // 2, g], got3.at[n % 2, i],
            gots3.at[i],
            ((s3.at[n, g], r3.at[n % 2, i]), (s3s.at[n // 2, g], r3s.at[i])), tm=to,
        )[: 1 + n % 2]

    def z_landed(p, i):
        return send(
            code3.at[p, pl.ds(0, orows), :], scale3.at[0, 0], got3.at[p, i - 1],
            gots3.at[i - 1],
            ((s3.at[p, 0], r3.at[p, i - 1]), (s3s.at[0, 0], r3s.at[i - 1])), tm=k ^ i,
        )

    def hop2(n):
        for m in (2 * n, 2 * n + 1):
            arrive(first_hop[m][1])
            for g in range(groups):
                v = keep[m, 1, group(g)] + unpack(got1.at[m, 1, group(g)], gots1.at[m, 1, g])
                pack(v, code2.at[m, group(g)], scale2.at[m, g])
            start(second_hop[m])

    def hop3(n):
        for b in range(2):
            m = 2 * n + b
            at = slice(cols * b, cols * (b + 1))
            arrive(first_hop[m][0])
            arrive(second_hop[m])
            for g in range(groups):
                v = (
                    keep[m, 0, group(g)]
                    + unpack(got1.at[m, 0, group(g)], gots1.at[m, 0, g])
                    + unpack(got2.at[m, group(g)], gots2.at[m, g])
                )
                plane[n, group(g), at] = v
                pack(v, code3.at[n, group(g), at], scale3.at[n // 2, g, :, pl.ds(2 * cols * (n % 2) + cols * b, cols)])
    def others(n, act, *targets):
        for g in targets:
            @pl.when(k != 4 * side(n // 2) + g)
            def _():
                act(z_send(n, g))

    def spread(n, *targets):
        others(n, start, *targets)

    def hop4(p):
        here = plane[2 * (early_side ^ (k // 4)) + p, pl.ds(pl.multiple_of(orows * (k % 4), orows), orows), :]
        there = None
        for i in (2, 4, 6, 1, 3, 5, 7):
            arrive(z_landed(p, i)[: 2 - p])
            v = unpack(got3.at[p, i - 1], gots3.at[i - 1, :, pl.ds(2 * cols * p, 2 * cols)])
            if i % 2 == 0:
                here = here + v
            else:
                there = v if there is None else there + v
        wide = 2 * cols
        o_ref[:, pl.ds(pl.multiple_of(half * j + wide * p, wide), wide)] = here * scale
        o_ref[:, pl.ds(pl.multiple_of(half * (1 - j) + wide * p, wide), wide)] = there * scale

    def products(n, go):
        u, p = n // 2, n % 2
        w = triple(u, p, hi, lo, hi_t, lo_t) + ext[u, p]
        for r in (3, 1, 2, 0):
            for b in range(2):
                m = 2 * n + b
                v = w[part * r : part * (r + 1), cols * b : cols * (b + 1)]
                if r == 3 or r == 1 + b:
                    slot = int(r == 3)
                    for g in range(groups):
                        pack(v[group(g)], code1.at[m, slot, group(g)], scale1.at[m, slot, g])
                    if slot in go:
                        start(first_hop[m][slot])
                else:
                    keep[m, int(r != 0)] = v

    def first(n, *slots):
        for slot in slots:
            for b in range(2):
                start(first_hop[2 * n + b][slot])

    def left(copies):
        for c_list in copies:
            leave(c_list)

    products(0, (0, 1))
    products(1, (0, 1))
    products(2, (1,))
    products(3, (1,))
    hop2(0)
    hop2(1)
    first(2, 0)
    hop2(2)
    first(3, 0)
    hop2(3)
    for cp in sum_copies:
        cp.wait_send()
    x_copy.wait_send()

    @pl.when((j == 1) & (z < 3))
    def _():
        for cp in ups:
            cp.wait_send()

    @pl.when((j == 0) & (z > 0))
    def _():
        for cp in downs:
            cp.wait_send()

    @pl.when(z > 0)
    def _():
        forwards[0].wait_send()

    @pl.when(z < 3)
    def _():
        forwards[1].wait_send()

    left((*first_hop[0], *first_hop[1]))
    left((*first_hop[2], *first_hop[3]))
    hop3(0)
    spread(0, 0, 1)
    hop3(1)
    spread(1, 0, 1)
    spread(0, 2, 3)
    spread(1, 2, 3)
    left((*first_hop[4], *first_hop[5]))
    left((*first_hop[6], *first_hop[7]))
    left((second_hop[0], second_hop[1]))
    left((second_hop[2], second_hop[3]))
    hop3(2)
    spread(2, 0, 1, 2, 3)
    hop3(3)
    spread(3, 0, 1, 2, 3)
    left((second_hop[4], second_hop[5]))
    left((second_hop[6], second_hop[7]))
    hop4(0)
    hop4(1)
    for n in range(NQ):
        others(n, leave, *range(groups))


def hbm(x):
    return pltpu.with_memory_space_constraint(x, pltpu.HBM)


def fused(traces, lengths):
    _, steps, width = traces.shape
    f32, bf16, i16 = jnp.float32, jnp.bfloat16, jnp.int16
    rows, cols = width // 4, width // 2 // NQ
    part, groups = rows // 2, 4
    dma = pltpu.SemaphoreType.DMA
    return pl.pallas_call(
        kernel,
        out_shape=jax.ShapeDtypeStruct((width // 32, width), f32),
        in_specs=[
            pl.BlockSpec(memory_space=pltpu.HBM),
            pl.BlockSpec(memory_space=pltpu.HBM),
        ],
        out_specs=pl.BlockSpec(memory_space=pltpu.VMEM),
        scratch_shapes=[
            pltpu.SMEM(lengths.shape, jnp.int32),
            pltpu.VMEM((3 * steps, width), bf16),
            pltpu.VMEM((2, NQ // 2, 2 * rows, 2 * cols), f32),
            pltpu.VMEM((3 * steps // 2, width), bf16),
            pltpu.VMEM((3 * steps // 2, width), bf16),
            pltpu.VMEM((width, 3 * steps // 2), bf16),
            pltpu.VMEM((width, 3 * steps // 2), bf16),
            pltpu.VMEM((8, 1, width), f32),
            pltpu.VMEM((steps, width), bf16),
            pltpu.VMEM((steps, width), bf16),
            pltpu.VMEM((width, steps), bf16),
            pltpu.VMEM((width, steps), bf16),
            pltpu.VMEM((2 * NQ, 2, part, cols), f32),
            pltpu.VMEM((2 * NQ, 2, part, cols), i16),
            pltpu.VMEM((2 * NQ, 2, groups, 1, cols), f32),
            pltpu.VMEM((2 * NQ, 2, part, cols), i16),
            pltpu.VMEM((2 * NQ, 2, groups, 1, cols), f32),
            pltpu.VMEM((2 * NQ, part, cols), i16),
            pltpu.VMEM((2 * NQ, groups, 1, cols), f32),
            pltpu.VMEM((2 * NQ, part, cols), i16),
            pltpu.VMEM((2 * NQ, groups, 1, cols), f32),
            pltpu.VMEM((NQ, part, 2 * cols), f32),
            pltpu.VMEM((NQ, part, 2 * cols), i16),
            pltpu.VMEM((2, groups, 1, 4 * cols), f32),
            pltpu.VMEM((2, 7, rows // 8, 2 * cols), i16),
            pltpu.VMEM((7, 1, 4 * cols), f32),
            pltpu.VMEM((1, width), f32),
            pltpu.VMEM((steps // 2, steps // 2), bf16),
            pltpu.VMEM((steps, 2 * steps), bf16),
            pltpu.VMEM((steps // 2, 3 * steps // 2), bf16),
            pltpu.VMEM((steps // 2, 3 * steps // 2), bf16),
            dma((2,)),
            dma((8,)), dma((8,)),
            dma, dma,
            dma((2,)), dma((2,)),
            dma((2,)), dma((2,)),
            dma((2 * NQ, 2)), dma((2 * NQ, 2)), dma((2 * NQ, 2)), dma((2 * NQ, 2)),
            dma((2 * NQ,)), dma((2 * NQ,)), dma((2 * NQ,)), dma((2 * NQ,)),
            dma((NQ, 4)), dma((2, 7)), dma((2, 4)), dma((7,)),
        ],
        compiler_params=pltpu.CompilerParams(
            collective_id=0, has_side_effects=True, vmem_limit_bytes=24 * 2**20
        ),
    )(hbm(lengths), hbm(traces.reshape(steps, width)))


def body(mesh, traces, lengths):
    chains, steps, width = traces.shape
    laid_out = (
        mesh.shape["groups"] == 1 and mesh.shape["chain"] == 4 and mesh.shape["tm"] == 8
    )
    if laid_out and chains == 1 and steps == LAG and width == 1024:
        return fused(traces, lengths)
    return on_device(traces, lengths)


def solution(mesh):
    in_specs = (P(("groups", "chain"), "tm", None), P("groups"))
    out_specs = P(("groups", "chain", "tm"), None)
    return jax.shard_map(
        functools.partial(body, mesh), mesh=mesh, in_specs=in_specs, out_specs=out_specs,
        check_vma=False,
    )
```

```python
import functools

import jax
import jax.numpy as jnp
from jax import lax
from jax.experimental import pallas as pl
from jax.experimental.pallas import tpu as pltpu
from jax.sharding import PartitionSpec as P

LAG = 256
MESH = pl.DeviceIdType.MESH


def shifted(block, axis, distance):
    devices = range(lax.axis_size(axis))
    route = [(i - distance, i) for i in devices if i - distance in devices]
    return lax.ppermute(block, axis, route)


def window_sums(current, previous):
    chains, steps, width = current.shape
    count = steps // LAG
    blocks = current.reshape(chains, count, LAG, width)
    earlier = jnp.concatenate([previous[:, None], blocks[:, :-1]], axis=1)
    index = jnp.arange(LAG)
    lower = index[None, :] <= index[:, None]
    upper = index[None, :] > index[:, None]
    lower_mat = lower.astype(jnp.float32)
    upper_mat = upper.astype(jnp.float32)
    result = jnp.einsum("ij,cbjp->cbip", lower_mat, blocks, precision=lax.Precision.HIGHEST)
    result = result + jnp.einsum(
        "ij,cbjp->cbip", upper_mat, earlier, precision=lax.Precision.HIGHEST
    )
    return result.reshape(chains, steps, width)


def gram_rows(filtered):
    chains, steps, width = filtered.shape
    flat = filtered.reshape(chains * steps, width)
    return jnp.einsum("tk,tp->kp", flat, flat, precision=lax.Precision.HIGHEST)


def on_device(traces, lengths):
    chains, steps, width = traces.shape
    own_len = lax.dynamic_slice_in_dim(lengths, lax.axis_index("chain") * chains, chains)
    first_time = lax.axis_index("tm") * steps
    times = first_time + jnp.arange(steps, dtype=jnp.int32)
    valid = (times[None, :] < own_len[:, None]).astype(jnp.float32)
    back_times = times - steps
    back_valid = ((back_times[None, :] >= 0) & (back_times[None, :] < own_len[:, None])).astype(
        jnp.float32
    )
    behind = shifted(traces, "tm", 1)
    data = traces.astype(jnp.float32) * valid[..., None]
    earlier = behind.astype(jnp.float32) * back_valid[..., None]
    totals = lax.psum(jnp.sum(data, axis=1), "tm")
    mean = totals / own_len.astype(jnp.float32)[:, None]
    scale = 1.0 / (LAG * jnp.sum(lengths).astype(jnp.float32))
    centered = window_sums(
        (data - mean[:, None, :]) * valid[..., None],
        (earlier - mean[:, None, :]) * back_valid[..., None],
    )
    return lax.psum_scatter(
        scale * gram_rows(centered), ("chain", "tm"), scatter_dimension=0, tiled=True
    )


def dot(a, b):
    return jnp.dot(a, b, preferred_element_type=jnp.float32)


NQ = 4
TOP = 32767.0


def kernel(
    len_hbm, x_hbm, o_ref, len_ref, data, ext, hi_e, lo_e, hi_et, lo_et, sums, hi, lo, hi_t, lo_t, keep, code1, scale1, got1,
    gots1, code2, scale2, got2, gots2, plane, code3, scale3, got3, gots3, mean_ref, band_first, band_own, band_low, band_high, in_sem, s_sum, r_sum, s_x, r_x,
    s_halo, r_halo, s_fwd, r_fwd, s1, r1, s1s,
    r1s, s2, r2, s2s, r2s, s3, r3, s3s, r3s,
):
    steps, width = x_hbm.shape
    pad = steps // 2
    half = width // 2
    cols = half // NQ
    rows = width // 4
    part = rows // 2
    orows = rows // 8
    c = lax.axis_index("chain")
    k = lax.axis_index("tm")
    z = k // 2
    j = k % 2

    def copy(src, dst, send, recv, **where):
        return pltpu.make_async_remote_copy(
            src_ref=src, dst_ref=dst, send_sem=send, recv_sem=recv, device_id=where,
            device_id_type=MESH,
        )

    def start(copies):
        for cp in copies:
            cp.start()

    def leave(copies):
        for cp in copies:
            cp.wait_send()

    def arrive(copies):
        for cp in copies:
            cp.wait_recv()

    own = pl.ds(pl.multiple_of(pad + steps * j, pad), steps)
    len_in = pltpu.make_async_copy(len_hbm, len_ref, in_sem.at[0])
    x_in = pltpu.make_async_copy(x_hbm, data.at[own, :], in_sem.at[1])
    len_in.start()
    x_in.start()
    barrier = pltpu.get_barrier_semaphore()
    for r in range(1, 8):
        pl.semaphore_signal(barrier, inc=1, device_id={"tm": k ^ r}, device_id_type=MESH)
    for r in (1, 2):
        pl.semaphore_signal(barrier, inc=1, device_id={"chain": c ^ r}, device_id_type=MESH)

    len_in.wait()
    length = len_ref[c]
    total_len = len_ref[0]
    for i in range(1, len_ref.shape[0]):
        total_len = total_len + len_ref[i]
    scale = 1.0 / (LAG * jnp.full((1, 1), total_len, jnp.int32).astype(jnp.float32))

    time = k * steps + lax.broadcasted_iota(jnp.int32, (steps, 1), 0)
    valid = (time < length).astype(jnp.float32)
    x_in.wait()
    sums[0] = jnp.sum(data[own, :].astype(jnp.float32) * valid, axis=0, keepdims=True)

    @pl.when(z == 0)
    def _():
        data[0:pad, :] = jnp.zeros((pad, width), data.dtype)

    @pl.when(z != 0)
    def _():
        for ref in (hi_e, lo_e):
            ref[0:pad, :] = jnp.zeros((pad, width), ref.dtype)
        for ref in (hi_et, lo_et):
            ref[:, 0:pad] = jnp.zeros((width, pad), ref.dtype)

    @pl.when(z == 3)
    def _():
        data[5 * pad : 6 * pad, :] = jnp.zeros((pad, width), data.dtype)

    pl.semaphore_wait(barrier, 9)

    sum_copies = [
        copy(sums.at[0], sums.at[r], s_sum.at[r], r_sum.at[r], tm=k ^ r) for r in range(1, 8)
    ]
    for cp in sum_copies:
        cp.start()
    def halo(way, h):
        near = 2 * jnp.minimum(z + 1, 3) if way == 0 else 2 * jnp.maximum(z - 1, 0)
        take = 4 * pad if way == 0 else pad
        put = 0 if way == 0 else 5 * pad
        at = pl.ds(half * h, half)
        return copy(
            data.at[pl.ds(take, pad), at], data.at[pl.ds(put, pad), at], s_halo.at[h],
            r_halo.at[way], tm=near + h,
        )

    ups = [halo(0, h) for h in range(2)]
    downs = [halo(1, h) for h in range(2)]

    @pl.when((j == 1) & (z < 3))
    def _():
        start(ups)

    @pl.when((j == 0) & (z > 0))
    def _():
        start(downs)

    x_copy = copy(data.at[own, :], data.at[own, :], s_x, r_x, tm=k ^ 1)
    x_copy.start()

    mine = pl.ds(pl.multiple_of(half * j, half), half)
    forwards, landed = [], []
    for way, put in ((0, 0), (1, 5 * pad)):
        block = data.at[pl.ds(put, pad), mine]
        forwards.append(copy(block, block, s_fwd.at[way], r_fwd.at[way], tm=k ^ 1))
        landed.append(copy(block, block, s_halo.at[0], r_halo.at[way], tm=k ^ 1))

    def set_band(band, when, begin):
        row = 2 * steps * z + when + lax.broadcasted_iota(jnp.int32, band.shape, 0)
        col = 2 * steps * z + begin - pad + lax.broadcasted_iota(jnp.int32, band.shape, 1)
        inside = (col > row - LAG) & (col <= row) & (col >= 0) & (col < length)
        band[...] = inside.astype(jnp.float32).astype(jnp.bfloat16)

    set_band(band_first, 0, pad)
    set_band(band_own, steps, pad)
    set_band(band_low, pad, 0)
    set_band(band_high, 2 * steps, 3 * pad)
    for cp in sum_copies:
        cp.wait_recv()
    total = sums[0]
    for r in range(1, 8):
        total = total + sums[r]
    mean_ref[...] = total / jnp.full((1, 1), length, jnp.int32).astype(jnp.float32)

    def split(w, b, outs, out):
        to_hi, to_lo, to_hi_t, to_lo_t = outs
        at = slice(rows * b, rows * (b + 1))
        h = w.astype(jnp.bfloat16)
        e = (w - h.astype(jnp.float32)).astype(jnp.bfloat16)
        to_hi[out, at] = h
        to_lo[out, at] = e
        h_t, e_t = h.T, e.T
        for u in range(2):
            to = pl.ds(pl.multiple_of(4 * part * u + part * (c ^ b), part), part)
            to_hi_t[to, out] = h_t[part * u : part * (u + 1)]
            to_lo_t[to, out] = e_t[part * u : part * (u + 1)]

    def windows(when, count, begin, span, band, outs, at_row, blocks=(0, 1, 2, 3)):
        t = 2 * steps * z + when + lax.broadcasted_iota(jnp.int32, (count, 1), 0)
        number = jnp.maximum(
            jnp.minimum(t + 1, length) - jnp.maximum(t - (LAG - 1), 0), 0
        ).astype(jnp.float32)
        for b in blocks:
            at = slice(rows * b, rows * (b + 1))
            w = dot(band[...], data[begin : begin + span, at]) - number * mean_ref[:, at]
            split(w, b, outs, slice(at_row, at_row + count))

    def forward():
        @pl.when(z > 0)
        def _():
            landed[0].wait_recv()
            forwards[0].start()

        @pl.when(z < 3)
        def _():
            landed[1].wait_recv()
            forwards[1].start()

    early_side = jnp.where(z == 0, 1, 0)

    def side(turn):
        return 1 - early_side if turn else early_side

    def triple(u, p, a_hi, a_lo, a_hi_t, a_lo_t):
        at = pl.ds(pl.multiple_of(half * j + 2 * cols * p, 2 * cols), 2 * cols)
        left = pl.ds(pl.multiple_of(4 * part * side(u), 4 * part), 4 * part)
        return (
            dot(a_hi_t[left, :], a_lo[:, at])
            + dot(a_lo_t[left, :], a_hi[:, at])
            + dot(a_hi_t[left, :], a_hi[:, at])
        )

    before = (hi_e, lo_e, hi_et, lo_et)
    after = (hi, lo, hi_t, lo_t)

    def early_products(u, p):
        ext[u, p] = triple(u, p, *before)

    x_copy.wait_recv()

    @pl.when(z == 0)
    def _():
        windows(0, pad, pad, pad, band_first, before, 0)

    windows(steps, steps, pad, 2 * steps, band_own, before, pad)
    pl.when(j == 0)(forward)
    early_products(0, 0)
    early_products(0, 1)
    early_products(1, 0)
    early_products(1, 1)
    pl.when(j == 1)(forward)

    @pl.when(z > 0)
    def _():
        forwards[0].wait_recv()

    windows(pad, pad, 0, 3 * pad, band_low, after, 0)

    @pl.when(z < 3)
    def _():
        forwards[1].wait_recv()

    windows(2 * steps, pad, 3 * pad, 3 * pad, band_high, after, pad)

    def send(codes, scales, to_codes, to_scales, sems, **where):
        (sc, rc), (ss, rs) = sems
        return [
            copy(codes, to_codes, sc, rc, **where),
            copy(scales, to_scales, ss, rs, **where),
        ]

    def pack(v, code, scale):
        top = jnp.maximum(jnp.max(jnp.abs(v), axis=0, keepdims=True), 1e-33)
        scale[...] = top * (1.0 / TOP)
        code[...] = jnp.round(v * (TOP / top)).astype(jnp.int32).astype(jnp.int16)

    def unpack(code, scale):
        return code[...].astype(jnp.int32).astype(jnp.float32) * scale[...]

    groups = part // orows

    def group(g):
        return slice(orows * g, orows * (g + 1))

    first_hop, second_hop = [], []
    for m in range(2 * NQ):
        m1 = 1 + m % 2
        codes = [
            copy(
                code1.at[m, i], got1.at[m, i], s1.at[m, i], r1.at[m, i], chain=c ^ m1,
            )
            for i in range(2)
        ]
        if m < NQ:
            scales = [
                copy(
                    scale1.at[m, i], gots1.at[m, i], s1s.at[m, i], r1s.at[m, i], chain=c ^ m1,
                )
                for i in range(2)
            ]
            first_hop.append([[codes[i], scales[i]] for i in range(2)])
        else:
            both = copy(scale1.at[m], gots1.at[m], s1s.at[m, 0], r1s.at[m, 0], chain=c ^ m1)
            first_hop.append([codes[:1], [codes[1], both]])
        second_hop.append(
            send(
                code2.at[m], scale2.at[m], got2.at[m], gots2.at[m],
                ((s2.at[m], r2.at[m]), (s2s.at[m], r2s.at[m])), chain=c ^ (3 - m1),
            )
        )

    def z_send(n, g):
        to = 4 * side(n // 2) + g
        i = jnp.maximum((k ^ to) - 1, 0)
        return send(
            code3.at[n, pl.ds(orows * g, orows), :], scale3.at[n // 2, g], got3.at[n % 2, i],
            gots3.at[i],
            ((s3.at[n, g], r3.at[n % 2, i]), (s3s.at[n // 2, g], r3s.at[i])), tm=to,
        )[: 1 + n % 2]

    def z_landed(p, i):
        return send(
            code3.at[p, pl.ds(0, orows), :], scale3.at[0, 0], got3.at[p, i - 1],
            gots3.at[i - 1],
            ((s3.at[p, 0], r3.at[p, i - 1]), (s3s.at[0, 0], r3s.at[i - 1])), tm=k ^ i,
        )

    def hop2(n):
        for m in (2 * n, 2 * n + 1):
            arrive(first_hop[m][1])
            for g in range(groups):
                v = keep[m, 1, group(g)] + unpack(got1.at[m, 1, group(g)], gots1.at[m, 1, g])
                pack(v, code2.at[m, group(g)], scale2.at[m, g])
            start(second_hop[m])

    def hop3(n):
        for b in range(2):
            m = 2 * n + b
            at = slice(cols * b, cols * (b + 1))
            arrive(first_hop[m][0])
            arrive(second_hop[m])
            for g in range(groups):
                v = (
                    keep[m, 0, group(g)]
                    + unpack(got1.at[m, 0, group(g)], gots1.at[m, 0, g])
                    + unpack(got2.at[m, group(g)], gots2.at[m, g])
                )
                plane[n, group(g), at] = v
                pack(v, code3.at[n, group(g), at], scale3.at[n // 2, g, :, pl.ds(2 * cols * (n % 2) + cols * b, cols)])
    def others(n, act, *targets):
        for g in targets:
            @pl.when(k != 4 * side(n // 2) + g)
            def _():
                act(z_send(n, g))

    def spread(n, *targets):
        others(n, start, *targets)

    def hop4(p):
        here = plane[2 * (early_side ^ (k // 4)) + p, pl.ds(pl.multiple_of(orows * (k % 4), orows), orows), :]
        there = None
        for i in (2, 4, 6, 1, 3, 5, 7):
            arrive(z_landed(p, i)[: 2 - p])
            v = unpack(got3.at[p, i - 1], gots3.at[i - 1, :, pl.ds(2 * cols * p, 2 * cols)])
            if i % 2 == 0:
                here = here + v
            else:
                there = v if there is None else there + v
        wide = 2 * cols
        o_ref[:, pl.ds(pl.multiple_of(half * j + wide * p, wide), wide)] = here * scale
        o_ref[:, pl.ds(pl.multiple_of(half * (1 - j) + wide * p, wide), wide)] = there * scale

    def products(n, go):
        u, p = n // 2, n % 2
        w = triple(u, p, hi, lo, hi_t, lo_t) + ext[u, p]
        for r in (3, 1, 2, 0):
            for b in range(2):
                m = 2 * n + b
                v = w[part * r : part * (r + 1), cols * b : cols * (b + 1)]
                if r == 3 or r == 1 + b:
                    slot = int(r == 3)
                    for g in range(groups):
                        pack(v[group(g)], code1.at[m, slot, group(g)], scale1.at[m, slot, g])
                    if slot in go:
                        start(first_hop[m][slot][: 2 if n < 2 else 1])
                else:
                    keep[m, int(r != 0)] = v
        for b in range(2):
            if n >= 2:
                start(first_hop[2 * n + b][1][1:])

    def first(n, *slots):
        for slot in slots:
            for b in range(2):
                start(first_hop[2 * n + b][slot])

    def left(copies):
        for c_list in copies:
            leave(c_list)

    products(0, (0, 1))
    products(1, (0, 1))
    products(2, (1,))
    products(3, (1,))
    hop2(0)
    hop2(1)
    first(2, 0)
    hop2(2)
    first(3, 0)
    hop2(3)
    for cp in sum_copies:
        cp.wait_send()
    x_copy.wait_send()

    @pl.when((j == 1) & (z < 3))
    def _():
        for cp in ups:
            cp.wait_send()

    @pl.when((j == 0) & (z > 0))
    def _():
        for cp in downs:
            cp.wait_send()

    @pl.when(z > 0)
    def _():
        forwards[0].wait_send()

    @pl.when(z < 3)
    def _():
        forwards[1].wait_send()

    left((*first_hop[0], *first_hop[1]))
    left((*first_hop[2], *first_hop[3]))
    hop3(0)
    spread(0, 0, 1)
    hop3(1)
    spread(1, 0, 1)
    spread(0, 2, 3)
    spread(1, 2, 3)
    left((*first_hop[4], *first_hop[5]))
    left((*first_hop[6], *first_hop[7]))
    left((second_hop[0], second_hop[1]))
    left((second_hop[2], second_hop[3]))
    hop3(2)
    spread(2, 0, 1, 2, 3)
    hop3(3)
    spread(3, 0, 1, 2, 3)
    left((second_hop[4], second_hop[5]))
    left((second_hop[6], second_hop[7]))
    hop4(0)
    hop4(1)
    for n in range(NQ):
        others(n, leave, *range(groups))


def hbm(x):
    return pltpu.with_memory_space_constraint(x, pltpu.HBM)


def fused(traces, lengths):
    _, steps, width = traces.shape
    f32, bf16, i16 = jnp.float32, jnp.bfloat16, jnp.int16
    rows, cols = width // 4, width // 2 // NQ
    part, groups = rows // 2, 4
    dma = pltpu.SemaphoreType.DMA
    return pl.pallas_call(
        kernel,
        out_shape=jax.ShapeDtypeStruct((width // 32, width), f32),
        in_specs=[
            pl.BlockSpec(memory_space=pltpu.HBM),
            pl.BlockSpec(memory_space=pltpu.HBM),
        ],
        out_specs=pl.BlockSpec(memory_space=pltpu.VMEM),
        scratch_shapes=[
            pltpu.SMEM(lengths.shape, jnp.int32),
            pltpu.VMEM((3 * steps, width), bf16),
            pltpu.VMEM((2, NQ // 2, 2 * rows, 2 * cols), f32),
            pltpu.VMEM((3 * steps // 2, width), bf16),
            pltpu.VMEM((3 * steps // 2, width), bf16),
            pltpu.VMEM((width, 3 * steps // 2), bf16),
            pltpu.VMEM((width, 3 * steps // 2), bf16),
            pltpu.VMEM((8, 1, width), f32),
            pltpu.VMEM((steps, width), bf16),
            pltpu.VMEM((steps, width), bf16),
            pltpu.VMEM((width, steps), bf16),
            pltpu.VMEM((width, steps), bf16),
            pltpu.VMEM((2 * NQ, 2, part, cols), f32),
            pltpu.VMEM((2 * NQ, 2, part, cols), i16),
            pltpu.VMEM((2 * NQ, 2, groups, 1, cols), f32),
            pltpu.VMEM((2 * NQ, 2, part, cols), i16),
            pltpu.VMEM((2 * NQ, 2, groups, 1, cols), f32),
            pltpu.VMEM((2 * NQ, part, cols), i16),
            pltpu.VMEM((2 * NQ, groups, 1, cols), f32),
            pltpu.VMEM((2 * NQ, part, cols), i16),
            pltpu.VMEM((2 * NQ, groups, 1, cols), f32),
            pltpu.VMEM((NQ, part, 2 * cols), f32),
            pltpu.VMEM((NQ, part, 2 * cols), i16),
            pltpu.VMEM((2, groups, 1, 4 * cols), f32),
            pltpu.VMEM((2, 7, rows // 8, 2 * cols), i16),
            pltpu.VMEM((7, 1, 4 * cols), f32),
            pltpu.VMEM((1, width), f32),
            pltpu.VMEM((steps // 2, steps // 2), bf16),
            pltpu.VMEM((steps, 2 * steps), bf16),
            pltpu.VMEM((steps // 2, 3 * steps // 2), bf16),
            pltpu.VMEM((steps // 2, 3 * steps // 2), bf16),
            dma((2,)),
            dma((8,)), dma((8,)),
            dma, dma,
            dma((2,)), dma((2,)),
            dma((2,)), dma((2,)),
            dma((2 * NQ, 2)), dma((2 * NQ, 2)), dma((2 * NQ, 2)), dma((2 * NQ, 2)),
            dma((2 * NQ,)), dma((2 * NQ,)), dma((2 * NQ,)), dma((2 * NQ,)),
            dma((NQ, 4)), dma((2, 7)), dma((2, 4)), dma((7,)),
        ],
        compiler_params=pltpu.CompilerParams(
            collective_id=0, has_side_effects=True, vmem_limit_bytes=24 * 2**20
        ),
    )(hbm(lengths), hbm(traces.reshape(steps, width)))


def body(mesh, traces, lengths):
    chains, steps, width = traces.shape
    laid_out = (
        mesh.shape["groups"] == 1 and mesh.shape["chain"] == 4 and mesh.shape["tm"] == 8
    )
    if laid_out and chains == 1 and steps == LAG and width == 1024:
        return fused(traces, lengths)
    return on_device(traces, lengths)


def solution(mesh):
    in_specs = (P(("groups", "chain"), "tm", None), P("groups"))
    out_specs = P(("groups", "chain", "tm"), None)
    return jax.shard_map(
        functools.partial(body, mesh), mesh=mesh, in_specs=in_specs, out_specs=out_specs,
        check_vma=False,
    )
```

```python
import functools

import jax
import jax.numpy as jnp
from jax import lax
from jax.experimental import pallas as pl
from jax.experimental.pallas import tpu as pltpu
from jax.sharding import PartitionSpec as P

LAG = 256
MESH = pl.DeviceIdType.MESH


def shifted(block, axis, distance):
    devices = range(lax.axis_size(axis))
    route = [(i - distance, i) for i in devices if i - distance in devices]
    return lax.ppermute(block, axis, route)


def window_sums(current, previous):
    chains, steps, width = current.shape
    count = steps // LAG
    blocks = current.reshape(chains, count, LAG, width)
    earlier = jnp.concatenate([previous[:, None], blocks[:, :-1]], axis=1)
    index = jnp.arange(LAG)
    lower = index[None, :] <= index[:, None]
    upper = index[None, :] > index[:, None]
    lower_mat = lower.astype(jnp.float32)
    upper_mat = upper.astype(jnp.float32)
    result = jnp.einsum("ij,cbjp->cbip", lower_mat, blocks, precision=lax.Precision.HIGHEST)
    result = result + jnp.einsum(
        "ij,cbjp->cbip", upper_mat, earlier, precision=lax.Precision.HIGHEST
    )
    return result.reshape(chains, steps, width)


def gram_rows(filtered):
    chains, steps, width = filtered.shape
    flat = filtered.reshape(chains * steps, width)
    return jnp.einsum("tk,tp->kp", flat, flat, precision=lax.Precision.HIGHEST)


def on_device(traces, lengths):
    chains, steps, width = traces.shape
    own_len = lax.dynamic_slice_in_dim(lengths, lax.axis_index("chain") * chains, chains)
    first_time = lax.axis_index("tm") * steps
    times = first_time + jnp.arange(steps, dtype=jnp.int32)
    valid = (times[None, :] < own_len[:, None]).astype(jnp.float32)
    back_times = times - steps
    back_valid = ((back_times[None, :] >= 0) & (back_times[None, :] < own_len[:, None])).astype(
        jnp.float32
    )
    behind = shifted(traces, "tm", 1)
    data = traces.astype(jnp.float32) * valid[..., None]
    earlier = behind.astype(jnp.float32) * back_valid[..., None]
    totals = lax.psum(jnp.sum(data, axis=1), "tm")
    mean = totals / own_len.astype(jnp.float32)[:, None]
    scale = 1.0 / (LAG * jnp.sum(lengths).astype(jnp.float32))
    centered = window_sums(
        (data - mean[:, None, :]) * valid[..., None],
        (earlier - mean[:, None, :]) * back_valid[..., None],
    )
    return lax.psum_scatter(
        scale * gram_rows(centered), ("chain", "tm"), scatter_dimension=0, tiled=True
    )


def dot(a, b):
    return jnp.dot(a, b, preferred_element_type=jnp.float32)


NQ = 4
TOP = 32767.0


def kernel(
    len_hbm, x_hbm, o_ref, len_ref, data, ext, hi_e, lo_e, hi_et, lo_et, sums, hi, lo, hi_t, lo_t, keep, code1, scale1, got1,
    gots1, code2, scale2, got2, gots2, plane, code3, scale3, got3, gots3, mean_ref, band_first, band_own, band_low, band_high, in_sem, s_sum, r_sum, s_x, r_x,
    s_halo, r_halo, s_fwd, r_fwd, s1, r1, s1s,
    r1s, s2, r2, s2s, r2s, s3, r3, s3s, r3s,
):
    steps, width = x_hbm.shape
    pad = steps // 2
    half = width // 2
    cols = half // NQ
    rows = width // 4
    part = rows // 2
    orows = rows // 8
    c = lax.axis_index("chain")
    k = lax.axis_index("tm")
    z = k // 2
    j = k % 2

    def copy(src, dst, send, recv, **where):
        return pltpu.make_async_remote_copy(
            src_ref=src, dst_ref=dst, send_sem=send, recv_sem=recv, device_id=where,
            device_id_type=MESH,
        )

    def start(copies):
        for cp in copies:
            cp.start()

    def leave(copies):
        for cp in copies:
            cp.wait_send()

    def arrive(copies):
        for cp in copies:
            cp.wait_recv()

    own = pl.ds(pl.multiple_of(pad + steps * j, pad), steps)
    len_in = pltpu.make_async_copy(len_hbm, len_ref, in_sem.at[0])
    x_in = pltpu.make_async_copy(x_hbm, data.at[own, :], in_sem.at[1])
    len_in.start()
    x_in.start()
    barrier = pltpu.get_barrier_semaphore()
    for r in range(1, 8):
        pl.semaphore_signal(barrier, inc=1, device_id={"tm": k ^ r}, device_id_type=MESH)
    for r in (1, 2):
        pl.semaphore_signal(barrier, inc=1, device_id={"chain": c ^ r}, device_id_type=MESH)

    len_in.wait()
    length = len_ref[c]
    total_len = len_ref[0]
    for i in range(1, len_ref.shape[0]):
        total_len = total_len + len_ref[i]
    scale = 1.0 / (LAG * jnp.full((1, 1), total_len, jnp.int32).astype(jnp.float32))

    time = k * steps + lax.broadcasted_iota(jnp.int32, (steps, 1), 0)
    valid = (time < length).astype(jnp.float32)
    x_in.wait()
    sums[0] = jnp.sum(data[own, :].astype(jnp.float32) * valid, axis=0, keepdims=True)

    @pl.when(z == 0)
    def _():
        data[0:pad, :] = jnp.zeros((pad, width), data.dtype)

    @pl.when(z != 0)
    def _():
        for ref in (hi_e, lo_e):
            ref[0:pad, :] = jnp.zeros((pad, width), ref.dtype)
        for ref in (hi_et, lo_et):
            ref[:, 0:pad] = jnp.zeros((width, pad), ref.dtype)

    @pl.when(z == 3)
    def _():
        data[5 * pad : 6 * pad, :] = jnp.zeros((pad, width), data.dtype)

    pl.semaphore_wait(barrier, 9)

    sum_copies = [
        copy(sums.at[0], sums.at[r], s_sum.at[r], r_sum.at[r], tm=k ^ r) for r in range(1, 8)
    ]
    for cp in sum_copies:
        cp.start()
    def halo(way, h):
        near = 2 * jnp.minimum(z + 1, 3) if way == 0 else 2 * jnp.maximum(z - 1, 0)
        take = 4 * pad if way == 0 else pad
        put = 0 if way == 0 else 5 * pad
        at = pl.ds(half * h, half)
        return copy(
            data.at[pl.ds(take, pad), at], data.at[pl.ds(put, pad), at], s_halo.at[h],
            r_halo.at[way], tm=near + h,
        )

    ups = [halo(0, h) for h in range(2)]
    downs = [halo(1, h) for h in range(2)]

    @pl.when((j == 1) & (z < 3))
    def _():
        start(ups)

    @pl.when((j == 0) & (z > 0))
    def _():
        start(downs)

    x_copy = copy(data.at[own, :], data.at[own, :], s_x, r_x, tm=k ^ 1)
    x_copy.start()

    mine = pl.ds(pl.multiple_of(half * j, half), half)
    forwards, landed = [], []
    for way, put in ((0, 0), (1, 5 * pad)):
        block = data.at[pl.ds(put, pad), mine]
        forwards.append(copy(block, block, s_fwd.at[way], r_fwd.at[way], tm=k ^ 1))
        landed.append(copy(block, block, s_halo.at[0], r_halo.at[way], tm=k ^ 1))

    def set_band(band, when, begin):
        row = 2 * steps * z + when + lax.broadcasted_iota(jnp.int32, band.shape, 0)
        col = 2 * steps * z + begin - pad + lax.broadcasted_iota(jnp.int32, band.shape, 1)
        inside = (col > row - LAG) & (col <= row) & (col >= 0) & (col < length)
        band[...] = inside.astype(jnp.float32).astype(jnp.bfloat16)

    set_band(band_first, 0, pad)
    set_band(band_own, steps, pad)
    set_band(band_low, pad, 0)
    set_band(band_high, 2 * steps, 3 * pad)
    for cp in sum_copies:
        cp.wait_recv()
    total = sums[0]
    for r in range(1, 8):
        total = total + sums[r]
    mean_ref[...] = total / jnp.full((1, 1), length, jnp.int32).astype(jnp.float32)

    def split(w, b, outs, out):
        to_hi, to_lo, to_hi_t, to_lo_t = outs
        at = slice(rows * b, rows * (b + 1))
        h = w.astype(jnp.bfloat16)
        e = (w - h.astype(jnp.float32)).astype(jnp.bfloat16)
        to_hi[out, at] = h
        to_lo[out, at] = e
        h_t, e_t = h.T, e.T
        for u in range(2):
            to = pl.ds(pl.multiple_of(4 * part * u + part * (c ^ b), part), part)
            to_hi_t[to, out] = h_t[part * u : part * (u + 1)]
            to_lo_t[to, out] = e_t[part * u : part * (u + 1)]

    def windows(when, count, begin, span, band, outs, at_row, blocks=(0, 1, 2, 3)):
        t = 2 * steps * z + when + lax.broadcasted_iota(jnp.int32, (count, 1), 0)
        number = jnp.maximum(
            jnp.minimum(t + 1, length) - jnp.maximum(t - (LAG - 1), 0), 0
        ).astype(jnp.float32)
        for b in blocks:
            at = slice(rows * b, rows * (b + 1))
            w = dot(band[...], data[begin : begin + span, at]) - number * mean_ref[:, at]
            split(w, b, outs, slice(at_row, at_row + count))

    def forward():
        @pl.when(z > 0)
        def _():
            landed[0].wait_recv()
            forwards[0].start()

        @pl.when(z < 3)
        def _():
            landed[1].wait_recv()
            forwards[1].start()

    early_side = jnp.where(z == 0, 1, 0)

    def side(turn):
        return 1 - early_side if turn else early_side

    def triple(u, p, a_hi, a_lo, a_hi_t, a_lo_t):
        at = pl.ds(pl.multiple_of(half * j + 2 * cols * p, 2 * cols), 2 * cols)
        left = pl.ds(pl.multiple_of(4 * part * side(u), 4 * part), 4 * part)
        return (
            dot(a_hi_t[left, :], a_lo[:, at])
            + dot(a_lo_t[left, :], a_hi[:, at])
            + dot(a_hi_t[left, :], a_hi[:, at])
        )

    before = (hi_e, lo_e, hi_et, lo_et)
    after = (hi, lo, hi_t, lo_t)

    def early_products(u, p):
        ext[u, p] = triple(u, p, *before)

    x_copy.wait_recv()

    @pl.when(z == 0)
    def _():
        windows(0, pad, pad, pad, band_first, before, 0)

    windows(steps, steps, pad, 2 * steps, band_own, before, pad)
    pl.when(j == 0)(forward)
    early_products(0, 0)
    early_products(0, 1)
    early_products(1, 0)
    early_products(1, 1)
    pl.when(j == 1)(forward)

    @pl.when(z > 0)
    def _():
        forwards[0].wait_recv()

    windows(pad, pad, 0, 3 * pad, band_low, after, 0)

    @pl.when(z < 3)
    def _():
        forwards[1].wait_recv()

    windows(2 * steps, pad, 3 * pad, 3 * pad, band_high, after, pad)

    def send(codes, scales, to_codes, to_scales, sems, **where):
        (sc, rc), (ss, rs) = sems
        return [
            copy(codes, to_codes, sc, rc, **where),
            copy(scales, to_scales, ss, rs, **where),
        ]

    def pack(v, code, scale):
        top = jnp.maximum(jnp.max(jnp.abs(v), axis=0, keepdims=True), 1e-33)
        scale[...] = top * (1.0 / TOP)
        code[...] = jnp.round(v * (TOP / top)).astype(jnp.int32).astype(jnp.int16)

    def unpack(code, scale):
        return code[...].astype(jnp.int32).astype(jnp.float32) * scale[...]

    groups = part // orows

    def group(g):
        return slice(orows * g, orows * (g + 1))

    first_hop, second_hop = [], []
    for m in range(2 * NQ):
        m1 = 1 + m % 2
        first_hop.append([
            send(
                code1.at[m, i], scale1.at[m, i], got1.at[m, i], gots1.at[m, i],
                ((s1.at[m, i], r1.at[m, i]), (s1s.at[m, i], r1s.at[m, i])), chain=c ^ m1,
            )
            for i in range(2)
        ])
        second_hop.append(
            send(
                code2.at[m], scale2.at[m], got2.at[m], gots2.at[m],
                ((s2.at[m], r2.at[m]), (s2s.at[m], r2s.at[m])), chain=c ^ (3 - m1),
            )
        )

    def z_send(n, g):
        to = 4 * side(n // 2) + g
        i = jnp.maximum((k ^ to) - 1, 0)
        return send(
            code3.at[n, pl.ds(orows * g, orows), :], scale3.at[n // 2, g], got3.at[n % 2, i],
            gots3.at[i],
            ((s3.at[n, g], r3.at[n % 2, i]), (s3s.at[n // 2, g], r3s.at[i])), tm=to,
        )[: 1 + n % 2]

    def z_landed(p, i):
        return send(
            code3.at[p, pl.ds(0, orows), :], scale3.at[0, 0], got3.at[p, i - 1],
            gots3.at[i - 1],
            ((s3.at[p, 0], r3.at[p, i - 1]), (s3s.at[0, 0], r3s.at[i - 1])), tm=k ^ i,
        )

    def hop2(n):
        for m in (2 * n, 2 * n + 1):
            arrive(first_hop[m][1])
            for g in range(groups):
                v = keep[m, 1, group(g)] + unpack(got1.at[m, 1, group(g)], gots1.at[m, 1, g])
                pack(v, code2.at[m, group(g)], scale2.at[m, g])
            start(second_hop[m])

    def hop3(n):
        for b in range(2):
            m = 2 * n + b
            at = slice(cols * b, cols * (b + 1))
            arrive(first_hop[m][0])
            arrive(second_hop[m])
            for g in range(groups):
                v = (
                    keep[m, 0, group(g)]
                    + unpack(got1.at[m, 0, group(g)], gots1.at[m, 0, g])
                    + unpack(got2.at[m, group(g)], gots2.at[m, g])
                )
                plane[n, group(g), at] = v
                pack(v, code3.at[n, group(g), at], scale3.at[n // 2, g, :, pl.ds(2 * cols * (n % 2) + cols * b, cols)])
    def others(n, act, *targets):
        for g in targets:
            @pl.when(k != 4 * side(n // 2) + g)
            def _():
                act(z_send(n, g))

    def spread(n, *targets):
        others(n, start, *targets)

    def hop4(p):
        here = plane[2 * (early_side ^ (k // 4)) + p, pl.ds(pl.multiple_of(orows * (k % 4), orows), orows), :]
        there = None
        for i in (2, 4, 6, 1, 3, 5, 7):
            arrive(z_landed(p, i)[: 2 - p])
            v = unpack(got3.at[p, i - 1], gots3.at[i - 1, :, pl.ds(2 * cols * p, 2 * cols)])
            if i % 2 == 0:
                here = here + v
            else:
                there = v if there is None else there + v
        wide = 2 * cols
        o_ref[:, pl.ds(pl.multiple_of(half * j + wide * p, wide), wide)] = here * scale
        o_ref[:, pl.ds(pl.multiple_of(half * (1 - j) + wide * p, wide), wide)] = there * scale

    def products(n, go):
        u, p = n // 2, n % 2
        w = triple(u, p, hi, lo, hi_t, lo_t) + ext[u, p]
        for r in (3, 1, 2, 0):
            for b in range(2):
                m = 2 * n + b
                v = w[part * r : part * (r + 1), cols * b : cols * (b + 1)]
                if r == 3 or r == 1 + b:
                    slot = int(r == 3)
                    for g in range(groups):
                        pack(v[group(g)], code1.at[m, slot, group(g)], scale1.at[m, slot, g])
                    if slot in go:
                        start(first_hop[m][slot])
                else:
                    keep[m, int(r != 0)] = v

    def first(n, *slots):
        for slot in slots:
            for b in range(2):
                start(first_hop[2 * n + b][slot])

    def left(copies):
        for c_list in copies:
            leave(c_list)

    products(0, (0, 1))
    products(1, (0, 1))
    products(2, (1,))
    products(3, (1,))
    hop2(0)
    hop2(1)
    first(2, 0)
    hop2(2)
    first(3, 0)
    hop2(3)
    for cp in sum_copies:
        cp.wait_send()
    x_copy.wait_send()

    @pl.when((j == 1) & (z < 3))
    def _():
        for cp in ups:
            cp.wait_send()

    @pl.when((j == 0) & (z > 0))
    def _():
        for cp in downs:
            cp.wait_send()

    @pl.when(z > 0)
    def _():
        forwards[0].wait_send()

    @pl.when(z < 3)
    def _():
        forwards[1].wait_send()

    left((*first_hop[0], *first_hop[1]))
    left((*first_hop[2], *first_hop[3]))
    hop3(0)
    spread(0, 0, 1)
    hop3(1)
    spread(1, 0, 1)
    spread(0, 2, 3)
    spread(1, 2, 3)
    left((*first_hop[4], *first_hop[5]))
    left((*first_hop[6], *first_hop[7]))
    left((second_hop[0], second_hop[1]))
    left((second_hop[2], second_hop[3]))
    hop3(2)
    spread(2, 0, 1, 2, 3)
    hop3(3)
    spread(3, 0, 1, 2, 3)
    hop4(0)
    hop4(1)
    left((second_hop[4], second_hop[5]))
    left((second_hop[6], second_hop[7]))
    for n in range(NQ):
        others(n, leave, *range(groups))


def hbm(x):
    return pltpu.with_memory_space_constraint(x, pltpu.HBM)


def fused(traces, lengths):
    _, steps, width = traces.shape
    f32, bf16, i16 = jnp.float32, jnp.bfloat16, jnp.int16
    rows, cols = width // 4, width // 2 // NQ
    part, groups = rows // 2, 4
    dma = pltpu.SemaphoreType.DMA
    return pl.pallas_call(
        kernel,
        out_shape=jax.ShapeDtypeStruct((width // 32, width), f32),
        in_specs=[
            pl.BlockSpec(memory_space=pltpu.HBM),
            pl.BlockSpec(memory_space=pltpu.HBM),
        ],
        out_specs=pl.BlockSpec(memory_space=pltpu.VMEM),
        scratch_shapes=[
            pltpu.SMEM(lengths.shape, jnp.int32),
            pltpu.VMEM((3 * steps, width), bf16),
            pltpu.VMEM((2, NQ // 2, 2 * rows, 2 * cols), f32),
            pltpu.VMEM((3 * steps // 2, width), bf16),
            pltpu.VMEM((3 * steps // 2, width), bf16),
            pltpu.VMEM((width, 3 * steps // 2), bf16),
            pltpu.VMEM((width, 3 * steps // 2), bf16),
            pltpu.VMEM((8, 1, width), f32),
            pltpu.VMEM((steps, width), bf16),
            pltpu.VMEM((steps, width), bf16),
            pltpu.VMEM((width, steps), bf16),
            pltpu.VMEM((width, steps), bf16),
            pltpu.VMEM((2 * NQ, 2, part, cols), f32),
            pltpu.VMEM((2 * NQ, 2, part, cols), i16),
            pltpu.VMEM((2 * NQ, 2, groups, 1, cols), f32),
            pltpu.VMEM((2 * NQ, 2, part, cols), i16),
            pltpu.VMEM((2 * NQ, 2, groups, 1, cols), f32),
            pltpu.VMEM((2 * NQ, part, cols), i16),
            pltpu.VMEM((2 * NQ, groups, 1, cols), f32),
            pltpu.VMEM((2 * NQ, part, cols), i16),
            pltpu.VMEM((2 * NQ, groups, 1, cols), f32),
            pltpu.VMEM((NQ, part, 2 * cols), f32),
            pltpu.VMEM((NQ, part, 2 * cols), i16),
            pltpu.VMEM((2, groups, 1, 4 * cols), f32),
            pltpu.VMEM((2, 7, rows // 8, 2 * cols), i16),
            pltpu.VMEM((7, 1, 4 * cols), f32),
            pltpu.VMEM((1, width), f32),
            pltpu.VMEM((steps // 2, steps // 2), bf16),
            pltpu.VMEM((steps, 2 * steps), bf16),
            pltpu.VMEM((steps // 2, 3 * steps // 2), bf16),
            pltpu.VMEM((steps // 2, 3 * steps // 2), bf16),
            dma((2,)),
            dma((8,)), dma((8,)),
            dma, dma,
            dma((2,)), dma((2,)),
            dma((2,)), dma((2,)),
            dma((2 * NQ, 2)), dma((2 * NQ, 2)), dma((2 * NQ, 2)), dma((2 * NQ, 2)),
            dma((2 * NQ,)), dma((2 * NQ,)), dma((2 * NQ,)), dma((2 * NQ,)),
            dma((NQ, 4)), dma((2, 7)), dma((2, 4)), dma((7,)),
        ],
        compiler_params=pltpu.CompilerParams(
            collective_id=0, has_side_effects=True, vmem_limit_bytes=24 * 2**20
        ),
    )(hbm(lengths), hbm(traces.reshape(steps, width)))


def body(mesh, traces, lengths):
    chains, steps, width = traces.shape
    laid_out = (
        mesh.shape["groups"] == 1 and mesh.shape["chain"] == 4 and mesh.shape["tm"] == 8
    )
    if laid_out and chains == 1 and steps == LAG and width == 1024:
        return fused(traces, lengths)
    return on_device(traces, lengths)


def solution(mesh):
    in_specs = (P(("groups", "chain"), "tm", None), P("groups"))
    out_specs = P(("groups", "chain", "tm"), None)
    return jax.shard_map(
        functools.partial(body, mesh), mesh=mesh, in_specs=in_specs, out_specs=out_specs,
        check_vma=False,
    )
```
